32 devices in a mesh: groups: 2 (over x), cols: 4 (over y, core), rows: 4 (over z).
Axes of the slice: x: 2, y: 2, z: 4, core: 2. Of those that a mesh axis runs over, the one named last changes fastest.
Arguments:
- camera_tokens: bfloat16 [1024, 6144], P(('groups', 'rows'), 'cols'), parts along dimension 0, may hold values from -150 to 150, as said below
- norm_gain: float32 [6144], P('cols'), may hold values from 0.25 to 1.75
- query_weight: bfloat16 [6144, 6144], P('cols', 'rows'), may hold values from -0.078125 to 0.078125
- key_weight: bfloat16 [6144, 6144], P('cols', 'rows'), may hold values from -0.078125 to 0.078125
- value_weight: bfloat16 [6144, 6144], P('cols', 'rows'), may hold values from -0.078125 to 0.078125
- query_gain: float32 [6144], P('rows'), may hold values from 0.5 to 14, as said below
- key_gain: float32 [6144], P('rows'), may hold values from 0.5 to 14, as said below
- out_weight: bfloat16 [6144, 6144], P('rows', 'cols'), may hold values from -0.078125 to 0.078125
- up_weight: bfloat16 [6144, 24576], P('cols', 'rows'), may hold values from -0.078125 to 0.078125
- up_bias: float32 [24576], P('rows'), may hold values from -3 to 3
- down_weight: bfloat16 [24576, 6144], P('rows', 'cols'), may hold values from -0.0390625 to 0.0390625
- down_bias: float32 [6144], P('cols'), may hold values from -3 to 3
- join_gain: float32 [6144], P('cols'), may hold values from 0.25 to 1.75
- join_query: bfloat16 [6144, 6144], P('cols', 'rows'), may hold values from -0.078125 to 0.078125
- join_key: bfloat16 [6144, 6144], P('cols', 'rows'), may hold values from -0.078125 to 0.078125
- join_value: bfloat16 [6144, 6144], P('cols', 'rows'), may hold values from -0.078125 to 0.078125
- join_query_gain: float32 [6144], P('rows'), may hold values from 0.5 to 14, as said below
- join_key_gain: float32 [6144], P('rows'), may hold values from 0.5 to 14, as said below
- join_out: bfloat16 [6144, 6144], P('rows', 'cols'), may hold values from -0.078125 to 0.078125
Outputs:
- joined_tokens: bfloat16 [1024, 6144], P(('groups', 'rows'), 'cols'), parts along dimension 0
The draws below stay inside these ranges and needn't reach their ends.
There are 2 independent parts, one for each index of `groups`. The reference program is written for one: setup_inputs(seed, part) draws one part's arguments, and reference() takes and returns one part's arrays. A program takes and returns all parts, laid end to end along the dimension named above; an argument that names none is the same for every part. Nothing has to cross between parts.
Inputs may be any that keep to these rules, and one draw needn't show every extreme that they name: `camera_tokens`: real valued tokens. `query_gain`: Positive. `key_gain`: Positive. `join_query_gain`: Positive. `join_key_gain`: Positive.
All inputs are finite; a program needn't handle non-finite values.
Results may differ from the reference program's by a relative error of at most 0.012.
Values may be sent and summed in bfloat16 or wider, within the bound.
A program may use at most 192 MiB of HBM per device.

```python
import math
import jax
import jax.numpy as jnp
from jax import lax

HEADS = 48
HEAD_DIM = 128
FF = 24576
CAMERAS = 8
TOK_CAM = 64
D = 6144
TOKENS = 512


def head_scales(key):
    subkeys = jax.random.split(key, 2)
    per_head = jnp.exp(jax.random.uniform(subkeys[0], (HEADS, 1), jnp.float32, math.log(1.2), math.log(3.5)))
    jitter = jax.random.uniform(subkeys[1], (HEADS, HEAD_DIM), jnp.float32, 0.8, 1.25)
    return (per_head * jitter).reshape(HEADS * HEAD_DIM)


def draw_query_gain(key, part):
    return head_scales(jax.random.fold_in(key, 11))


def draw_key_gain(key, part):
    return head_scales(jax.random.fold_in(key, 23))


def draw_join_query_gain(key, part):
    return head_scales(jax.random.fold_in(key, 37))


def draw_join_key_gain(key, part):
    return head_scales(jax.random.fold_in(key, 41))


def draw_camera_tokens(key, part):
    subkeys = jax.random.split(jax.random.fold_in(key, 5), 3)
    width = HEADS * HEAD_DIM
    gaussian = jax.random.truncated_normal(subkeys[0], -4.0, 4.0, (TOKENS, width), jnp.float32)
    rising = 3.0 ** (jnp.arange(width, dtype=jnp.float32) / width)
    row_scale = jnp.exp(jax.random.uniform(subkeys[1], (TOKENS, 1), jnp.float32, math.log(0.5), math.log(2.0)))
    col_scale = jnp.exp(jax.random.uniform(subkeys[2], (1, width), jnp.float32, math.log(0.6), math.log(1.6))) * rising
    return (gaussian * row_scale * col_scale).astype(jnp.bfloat16)


def levels(own_key, shape, shards, low, top_value):
    loudness = 1.0
    for dim, shards_of in shards:
        steps = jax.random.uniform(jax.random.fold_in(jax.random.fold_in(own_key, 6), dim), (shards_of,), jnp.float32, low / len(shards), top_value / len(shards))
        loudness = loudness * jnp.repeat(jnp.exp(steps), shape[dim] // shards_of).reshape((-1,) + (1,) * (len(shape) - 1 - dim))
    return loudness


def noise(own_key, extent, scale, most, cuts=(), kind=jnp.bfloat16):
    drawn = scale * jax.random.normal(own_key, extent, jnp.float32)
    if cuts:
        drawn = drawn * levels(own_key, extent, cuts, -0.22, 0.18)
    return jnp.clip(drawn, -most, most).astype(kind)


def setup_inputs(seed: int = 0, part: int = 0) -> dict:
    arg_keys = jax.random.split(jax.random.key(seed), 20)
    part_keys = jax.random.split(jax.random.fold_in(arg_keys[19], part), 20)
    return {
        "camera_tokens": draw_camera_tokens(jax.random.fold_in(jax.random.fold_in(arg_keys[19], part), 71), part),
        "norm_gain": jnp.clip(1.0 + 0.15 * jax.random.normal(arg_keys[1], (D,), jnp.float32), 0.25, 1.75),
        "query_weight": noise(arg_keys[2], (D, D), D ** -0.5, 0.078125, ((0, 4), (1, 4))),
        "key_weight": noise(arg_keys[3], (D, D), D ** -0.5, 0.078125, ((0, 4), (1, 4))),
        "value_weight": noise(arg_keys[4], (D, D), D ** -0.5, 0.078125, ((0, 4), (1, 4))),
        "query_gain": draw_query_gain(jax.random.fold_in(arg_keys[19], 71), part),
        "key_gain": draw_key_gain(jax.random.fold_in(arg_keys[19], 71), part),
        "out_weight": noise(arg_keys[7], (D, D), D ** -0.5, 0.078125, ((0, 4), (1, 4))),
        "up_weight": noise(arg_keys[8], (D, FF), D ** -0.5, 0.078125, ((0, 4), (1, 4))),
        "up_bias": noise(arg_keys[9], (FF,), 0.5, 3.0, ((0, 4),), jnp.float32),
        "down_weight": noise(arg_keys[10], (FF, D), FF ** -0.5, 0.0390625, ((0, 4), (1, 4))),
        "down_bias": noise(arg_keys[11], (D,), 0.5, 3.0, ((0, 4),), jnp.float32),
        "join_gain": jnp.clip(1.0 + 0.15 * jax.random.normal(arg_keys[12], (D,), jnp.float32), 0.25, 1.75),
        "join_query": noise(arg_keys[13], (D, D), D ** -0.5, 0.078125, ((0, 4), (1, 4))),
        "join_key": noise(arg_keys[14], (D, D), D ** -0.5, 0.078125, ((0, 4), (1, 4))),
        "join_value": noise(arg_keys[15], (D, D), D ** -0.5, 0.078125, ((0, 4), (1, 4))),
        "join_query_gain": draw_join_query_gain(jax.random.fold_in(arg_keys[19], 71), part),
        "join_key_gain": draw_join_key_gain(jax.random.fold_in(arg_keys[19], 71), part),
        "join_out": noise(arg_keys[18], (D, D), D ** -0.5, 0.078125, ((0, 4), (1, 4))),
    }


EPS = 1e-06

def layer_norm(values, scales):
    row_mean = lax.optimization_barrier(jnp.mean(values, -1, keepdims=True))
    row_var = lax.optimization_barrier(jnp.mean(values * values, -1, keepdims=True)) - row_mean * row_mean
    return ((values - row_mean) * lax.rsqrt(row_var + EPS) * scales).astype(jnp.bfloat16)

def head_norm(values, scales):
    row_count = values.shape[0]
    grouped = values.reshape(row_count, -1, HEAD_DIM)
    row_mean = lax.optimization_barrier(jnp.mean(grouped, -1, keepdims=True))
    row_var = lax.optimization_barrier(jnp.mean(grouped * grouped, -1, keepdims=True)) - row_mean * row_mean
    normed = (grouped - row_mean) * lax.rsqrt(row_var + EPS)
    return (normed.reshape(row_count, -1) * scales).astype(jnp.bfloat16)

def attend(queries, key_rows, val_rows):
    inv_root = 1.0 / math.sqrt(HEAD_DIM)
    scores = jnp.einsum('bqhd,bkhd->bhqk', queries.astype(jnp.float32), key_rows.astype(jnp.float32)) * inv_root
    row_max = lax.optimization_barrier(jnp.max(scores, -1, keepdims=True))
    weights = jnp.exp(scores - row_max)
    row_sum = lax.optimization_barrier(jnp.sum(weights, -1))
    rounded = lax.optimization_barrier(weights.astype(jnp.bfloat16)).astype(jnp.float32)
    blended = jnp.einsum('bhqk,bkhd->bqhd', rounded, val_rows.astype(jnp.float32))
    return blended / jnp.transpose(row_sum, (0, 2, 1))[..., None]

def reference(camera_tokens, norm_gain, query_weight, key_weight, value_weight, query_gain, key_gain, out_weight, up_weight, up_bias, down_weight, down_bias, join_gain, join_query, join_key, join_value, join_query_gain, join_key_gain, join_out):
    start_f32 = camera_tokens.astype(jnp.float32)
    normed = layer_norm(start_f32, norm_gain)
    query_raw = jnp.dot(normed, query_weight, preferred_element_type=jnp.float32)
    key_raw = jnp.dot(normed, key_weight, preferred_element_type=jnp.float32)
    value_raw = jnp.dot(normed, value_weight, preferred_element_type=jnp.float32)
    up_raw = jnp.dot(normed, up_weight, preferred_element_type=jnp.float32)
    query_normed = head_norm(query_raw, query_gain)
    key_normed = head_norm(key_raw, key_gain)
    value_rounded = value_raw.astype(jnp.bfloat16)
    cam_shape = (CAMERAS, TOK_CAM, HEADS, HEAD_DIM)
    attended = attend(query_normed.reshape(cam_shape), key_normed.reshape(cam_shape), value_rounded.reshape(cam_shape))
    attended = attended.reshape(TOKENS, D).astype(jnp.bfloat16)
    hidden = jax.nn.gelu(up_raw + up_bias, approximate=False).astype(jnp.bfloat16)
    mixed = jnp.dot(attended, out_weight, preferred_element_type=jnp.float32) + jnp.dot(hidden, down_weight, preferred_element_type=jnp.float32)
    camera_out = (start_f32 + mixed + down_bias).astype(jnp.bfloat16)
    layer_f32 = camera_out.astype(jnp.float32)
    join_normed = layer_norm(layer_f32, join_gain)
    join_q = head_norm(jnp.dot(join_normed, join_query, preferred_element_type=jnp.float32), join_query_gain)
    join_k = head_norm(jnp.dot(join_normed, join_key, preferred_element_type=jnp.float32), join_key_gain)
    join_v = jnp.dot(join_normed, join_value, preferred_element_type=jnp.float32).astype(jnp.bfloat16)
    all_shape = (1, TOKENS, HEADS, HEAD_DIM)
    join_attended = attend(join_q.reshape(all_shape), join_k.reshape(all_shape), join_v.reshape(all_shape))
    join_attended = join_attended.reshape(TOKENS, D).astype(jnp.bfloat16)
    return (layer_f32 + jnp.dot(join_attended, join_out, preferred_element_type=jnp.float32)).astype(jnp.bfloat16)
```

```python
import functools
import math

import jax
import jax.numpy as jnp
from jax import lax
from jax.experimental import pallas as pl
from jax.experimental.pallas import tpu as pltpu
from jax.sharding import PartitionSpec as P

HEAD_DIM = 128
TOK_CAM = 64
D = 6144


EPS = 1e-06


def partner_2(array, axis, bit):
    return lax.ppermute(array, axis, [(i, i ^ 1 << bit) for i in range(lax.axis_size(axis))])


def normalize(values, scales, moments):
    row_mean = moments[0] / D
    row_var = moments[1] / D - row_mean * row_mean
    return ((values - row_mean[:, None]) * lax.rsqrt(row_var[:, None] + EPS) * scales).astype(
        jnp.bfloat16
    )


def shard_moments(values):
    return lax.psum((jnp.sum(values, 1), jnp.sum(values * values, 1)), "cols")


def head_norm(values, scales):
    row_count = values.shape[0]
    grouped = values.reshape(row_count, -1, HEAD_DIM)
    row_mean = jnp.mean(grouped, -1, keepdims=True)
    row_var = jnp.mean(grouped * grouped, -1, keepdims=True) - row_mean * row_mean
    normed = (grouped - row_mean) * lax.rsqrt(row_var + EPS)
    return (normed.reshape(row_count, -1) * scales).astype(jnp.bfloat16)


def attend(queries, key_rows, val_rows):
    inv_root = 1.0 / math.sqrt(HEAD_DIM)
    scores = (
        jnp.einsum("bqhd,bkhd->bhqk", queries, key_rows, preferred_element_type=jnp.float32)
        * inv_root
    )
    row_max = jnp.max(scores, -1, keepdims=True)
    weights = jnp.exp(scores - row_max)
    row_sum = jnp.sum(weights, -1)
    blended = jnp.einsum(
        "bhqk,bkhd->bqhd",
        weights.astype(jnp.bfloat16),
        val_rows,
        preferred_element_type=jnp.float32,
    )
    return blended / jnp.transpose(row_sum, (0, 2, 1))[..., None]


def to_heads(matrix, blocks):
    return matrix.reshape(blocks, -1, matrix.shape[1] // HEAD_DIM, HEAD_DIM)


def camera_attention(queries, key_rows, val_rows):
    local_rows = queries.shape[0]
    if local_rows >= TOK_CAM:
        blocks = local_rows // TOK_CAM
        result = attend(
            to_heads(queries, blocks), to_heads(key_rows, blocks), to_heads(val_rows, blocks)
        )
    else:
        cam_span = TOK_CAM // local_rows
        position = lax.axis_index("cols")
        key_value = jnp.stack((key_rows, val_rows))
        for which_bit in range(cam_span.bit_length() - 1):
            partner = partner_2(key_value, "cols", which_bit)
            is_lower = position >> which_bit & 1 == 0
            key_value = jnp.where(
                is_lower,
                jnp.concatenate((key_value, partner), 1),
                jnp.concatenate((partner, key_value), 1),
            )
        result = attend(to_heads(queries, 1), to_heads(key_value[0], 1), to_heads(key_value[1], 1))
    return result.reshape(local_rows, -1).astype(jnp.bfloat16)


def plain_body(
    camera_tokens,
    norm_gain,
    query_weight,
    key_weight,
    value_weight,
    query_gain,
    key_gain,
    out_weight,
    up_weight,
    up_bias,
    down_weight,
    down_bias,
    join_gain,
    join_query,
    join_key,
    join_value,
    join_query_gain,
    join_key_gain,
    join_out,
):
    own_rows = camera_tokens.shape[0]
    all_rows = own_rows * lax.axis_size("rows")
    col_rows = all_rows // lax.axis_size("cols")
    attn_width = query_weight.shape[1]
    start_f32 = camera_tokens.astype(jnp.float32)
    normed_all = lax.all_gather(
        normalize(start_f32, norm_gain, shard_moments(start_f32)), "rows", axis=0, tiled=True
    )
    joint_weight = jnp.concatenate((query_weight, key_weight, value_weight, up_weight), 1)
    joint = lax.psum_scatter(
        jnp.dot(normed_all, joint_weight, preferred_element_type=jnp.float32),
        "cols",
        scatter_dimension=0,
        tiled=True,
    )
    up_sum = joint[:, 3 * attn_width :]
    hidden = jax.nn.gelu(up_sum + up_bias, approximate=False).astype(jnp.bfloat16)
    attended = camera_attention(
        head_norm(joint[:, :attn_width], query_gain),
        head_norm(joint[:, attn_width : 2 * attn_width], key_gain),
        joint[:, 2 * attn_width : 3 * attn_width].astype(jnp.bfloat16),
    )
    attn_all, hidden_all = (
        lax.all_gather(attended, "cols", axis=0, tiled=True),
        lax.all_gather(hidden, "cols", axis=0, tiled=True),
    )
    mixed = lax.psum_scatter(
        jnp.dot(attn_all, out_weight, preferred_element_type=jnp.float32)
        + jnp.dot(hidden_all, down_weight, preferred_element_type=jnp.float32),
        "rows",
        scatter_dimension=0,
        tiled=True,
    )
    layer_own = (start_f32 + mixed + down_bias).astype(jnp.bfloat16)
    layer_f32 = layer_own.astype(jnp.float32)
    join_in = lax.all_gather(
        normalize(layer_f32, join_gain, shard_moments(layer_f32)), "rows", axis=0, tiled=True
    )
    join_weight = jnp.concatenate((join_query, join_key, join_value), 1)
    join_joint = lax.psum_scatter(
        jnp.dot(join_in, join_weight, preferred_element_type=jnp.float32),
        "cols",
        scatter_dimension=0,
        tiled=True,
    )
    join_q = head_norm(join_joint[:, :attn_width], join_query_gain)
    join_k = head_norm(join_joint[:, attn_width : 2 * attn_width], join_key_gain)
    join_v = join_joint[:, 2 * attn_width :].astype(jnp.bfloat16)
    heads_here = attn_width // HEAD_DIM
    query_heads = join_q.reshape(col_rows, heads_here, HEAD_DIM)
    inv_root = 1.0 / math.sqrt(HEAD_DIM)
    run_max = jnp.full((heads_here, col_rows), -jnp.inf, jnp.float32)
    run_sum = jnp.zeros((heads_here, col_rows), jnp.float32)
    accum = jnp.zeros((col_rows, heads_here, HEAD_DIM), jnp.float32)
    key_part = lax.all_gather(join_k, "cols", axis=0, tiled=True)
    val_part = lax.all_gather(join_v, "cols", axis=0, tiled=True)
    row_count = key_part.shape[0]
    key_heads = key_part.reshape(row_count, heads_here, HEAD_DIM)
    val_heads = val_part.reshape(row_count, heads_here, HEAD_DIM)
    scores = (
        jnp.einsum("qhd,khd->hqk", query_heads, key_heads, preferred_element_type=jnp.float32)
        * inv_root
    )
    new_max = jnp.max(scores, -1)
    factor = jnp.exp(run_max - new_max)
    weights = jnp.exp(scores - new_max[..., None])
    run_sum = run_sum * factor + jnp.sum(weights, -1)
    accum = accum * jnp.transpose(factor)[..., None] + jnp.einsum(
        "hqk,khd->qhd", weights.astype(jnp.bfloat16), val_heads, preferred_element_type=jnp.float32
    )
    run_max, run_sum, accum = (new_max, run_sum, accum)
    joined_attn = (
        (accum / jnp.transpose(run_sum)[..., None])
        .reshape(col_rows, attn_width)
        .astype(jnp.bfloat16)
    )
    joined_all = lax.all_gather(joined_attn, "cols", axis=0, tiled=True)
    result = lax.psum_scatter(
        jnp.dot(joined_all, join_out, preferred_element_type=jnp.float32),
        "rows",
        scatter_dimension=0,
        tiled=True,
    )
    return (layer_own.astype(jnp.float32) + result).astype(jnp.bfloat16)


F32 = jnp.float32
BF16 = jnp.bfloat16
MESH = pl.DeviceIdType.MESH
VMEM_LIMIT = 66 * 1024 * 1024 - 3 * 1024 * 1024


def each(count, step):
    lax.fori_loop(0, count, lambda i, carry: (step(i), carry)[1], None)


def remote(src, dst, send, recv, device):
    return pltpu.make_async_remote_copy(
        src_ref=src,
        dst_ref=dst,
        send_sem=send,
        recv_sem=recv,
        device_id=device,
        device_id_type=MESH,
    )


def places():
    col = lax.axis_index("cols")
    core = lax.rem(col, 2)
    return col, col + 1 - 2 * core, lax.rem(col + 2, 4)


def greet(cols_away):
    col, row, row_count = lax.axis_index("cols"), lax.axis_index("rows"), lax.axis_size("rows")
    barrier = pltpu.get_barrier_semaphore()
    _, mate, across = places()
    others = {1: mate, 2: across}
    if cols_away == 3:
        others[3] = mate + across - col
    for other in others.values():
        pl.semaphore_signal(barrier, inc=1, device_id={"cols": other}, device_id_type=MESH)

    @pl.when(row > 0)
    def _():
        pl.semaphore_signal(barrier, inc=1, device_id={"rows": row - 1}, device_id_type=MESH)

    @pl.when(row < row_count - 1)
    def _():
        pl.semaphore_signal(barrier, inc=1, device_id={"rows": row + 1}, device_id_type=MESH)

    inner = (row > 0) & (row < row_count - 1)

    @pl.when(inner)
    def _():
        pl.semaphore_wait(barrier, len(others) + 2)

    @pl.when(jnp.logical_not(inner))
    def _():
        pl.semaphore_wait(barrier, len(others) + 1)


def gather_rows(normed, send_r, send_l, arrive):
    row, row_count = lax.axis_index("rows"), lax.axis_size("rows")

    def to_right(block):
        return remote(
            normed.at[block], normed.at[block], send_r.at[block], arrive.at[block], {"rows": row + 1}
        )

    def to_left(block):
        return remote(
            normed.at[block], normed.at[block], send_l.at[block], arrive.at[block], {"rows": row - 1}
        )

    def pass_on(from_left, block):
        if from_left:

            @pl.when(row < row_count - 1)
            def _():
                to_right(block).start()
        else:

            @pl.when(row > 0)
            def _():
                to_left(block).start()

    pass_on(True, row)
    pass_on(False, row)
    for away in range(1, row_count):

        @pl.when(row >= away)
        def _():
            to_right(row - away).wait_recv()
            pass_on(True, row - away)

        @pl.when(row + away < row_count)
        def _():
            to_left(row + away).wait_recv()
            pass_on(False, row + away)

    def finish():
        for block in range(row_count):

            @pl.when((row >= block) & (row < row_count - 1))
            def _():
                to_right(block).wait_send()

            @pl.when((row <= block) & (row > 0))
            def _():
                to_left(block).wait_send()

    return finish


def norm_heads(values, scales):
    parts = []
    for start in range(0, values.shape[1], HEAD_DIM):
        part = values[:, start : start + HEAD_DIM]
        mean = jnp.mean(part, -1, keepdims=True)
        var = jnp.mean(part * part, -1, keepdims=True) - mean * mean
        parts.append((part - mean) * lax.rsqrt(var + EPS))
    return (jnp.concatenate(parts, 1) * scales).astype(BF16)


def soft_blend(query, keys, values):
    scores = lax.dot_general(
        query, keys, (((1,), (1,)), ((), ())), preferred_element_type=F32
    ) * (1.0 / math.sqrt(HEAD_DIM))
    weights = jnp.exp(scores - jnp.max(scores, -1, keepdims=True))
    total = jnp.sum(weights, -1, keepdims=True)
    blended = jnp.dot(weights.astype(BF16), values, preferred_element_type=F32)
    return (blended / total).astype(BF16)


def in_kernel(span, has_up, width, *refs):
    refs = list(refs)
    tokens, gain, q_gain, k_gain, wq, wk, wv = refs[:7]
    refs = refs[7:]
    if has_up:
        bias, w_up = refs[:2]
        refs = refs[2:]
    out_a = refs.pop(0)
    if has_up:
        out_u = refs.pop(0)
    normed, moments, m_send, m_recv, z_right, z_left, z_arrive, queries, keys, values = refs[:10]
    groups = [refs[10:21]]
    if has_up:
        groups.append(refs[21:32])
    col, mate, across = places()
    diagonal = mate + across - col
    row, row_count = lax.axis_index("rows"), lax.axis_size("rows")
    own_rows = tokens.shape[0]

    def load(group, unit, owner, source, start):
        held = group[0]
        columns = pl.ds(pl.multiple_of(start, HEAD_DIM), held.shape[-1])
        return pltpu.make_async_copy(
            source.at[:, columns], held.at[unit * 4 + owner], group[6].at[unit * 4 + owner]
        )

    def loads(group_id, unit, owner, which=None):
        group = groups[group_id]
        wide = group[0].shape[-1]
        if group_id == 0:
            return load(group, unit, owner, (wq, wk, wv)[which], owner * wide)
        return load(group, unit, owner, w_up, owner * (groups[1][5].shape[0] * wide) + unit * wide)

    def start_loads(owner):
        for which in range(3):
            loads(0, which, owner, which).start()
        if has_up:
            each(groups[1][5].shape[0], lambda unit: loads(1, unit, owner).start())

    order = (diagonal, across, mate, col)
    for owner in order:
        start_loads(owner)
    greet(3)

    own = tokens[...].astype(F32)
    lane = lax.broadcasted_iota(jnp.int32, (own_rows, HEAD_DIM), 1)
    mine = jnp.where(
        lane < HEAD_DIM // 2,
        jnp.sum(own, 1, keepdims=True),
        jnp.sum(own * own, 1, keepdims=True),
    )
    moments[3] = mine
    swaps = []
    for slot, other in enumerate((mate, across, diagonal)):
        swap = remote(
            moments.at[3], moments.at[slot], m_send.at[slot], m_recv.at[slot], {"cols": other}
        )
        swap.start()
        swaps.append(swap)
    for swap in swaps:
        swap.wait_recv()
    total = (moments[3] + moments[0]) + (moments[1] + moments[2])
    mean = total[:, :1] / width
    var = total[:, HEAD_DIM // 2 : HEAD_DIM // 2 + 1] / width - mean * mean
    normed[row] = ((own - mean) * lax.rsqrt(var + EPS) * gain[...]).astype(BF16)
    finish_rows = gather_rows(normed, z_right, z_left, z_arrive)
    for swap in swaps:
        swap.wait_send()

    def ops(group):
        held, p_send, p_recv, y_send, y_recv, own_sum, _, ps, pr, ys, yr = group

        def product(unit, owner):
            weight = held.at[unit * 4 + owner]
            pltpu.make_async_copy(weight, weight, group[6].at[unit * 4 + owner]).wait()
            left = normed[...].reshape(row_count * own_rows, normed.shape[-1])
            return jnp.dot(left, weight[...], preferred_element_type=F32)

        def to_mate(half, unit):
            return remote(
                p_send.at[half, unit],
                p_recv.at[half, unit],
                ps.at[half, unit],
                pr.at[half, unit],
                {"cols": mate},
            )

        def to_across(unit):
            return remote(
                y_send.at[unit], y_recv.at[unit], ys.at[unit], yr.at[unit], {"cols": across}
            )

        def first(unit):
            p_send[0, unit] = product(unit, diagonal).astype(BF16)
            to_mate(0, unit).start()
            partial = product(unit, across)
            to_mate(0, unit).wait_recv()
            y_send[unit] = (partial + p_recv[0, unit].astype(F32)).astype(BF16)
            to_across(unit).start()

        def second(unit):
            p_send[1, unit] = product(unit, mate).astype(BF16)
            to_mate(1, unit).start()
            partial = product(unit, col)
            to_mate(1, unit).wait_recv()
            own_sum[unit] = partial + p_recv[1, unit].astype(F32)

        def final(unit):
            to_across(unit).wait_recv()
            return own_sum[unit] + y_recv[unit].astype(F32)

        def finish(unit):
            to_mate(0, unit).wait_send()
            to_mate(1, unit).wait_send()
            to_across(unit).wait_send()

        return first, second, final, finish, own_sum.shape[0]

    all_ops = [ops(group) for group in groups]
    for first, second, final, finish, count in all_ops:
        each(count, first)
    for first, second, final, finish, count in all_ops:
        each(count, second)
    final = all_ops[0][2]
    wide = groups[0][0].shape[-1]
    mine = pl.ds(pl.multiple_of(col * wide, HEAD_DIM), wide)
    queries[...] = norm_heads(final(0), q_gain[:, mine])
    keys[...] = norm_heads(final(1), k_gain[:, mine])
    values[...] = final(2).astype(BF16)

    def camera(which):
        rows = pl.ds(pl.multiple_of(which * span, span), span)
        for start in range(0, wide, HEAD_DIM):
            head = slice(start, start + HEAD_DIM)
            out_a[rows, head] = soft_blend(queries[rows, head], keys[rows, head], values[rows, head])

    each(out_a.shape[0] // span, camera)
    if has_up:
        final = all_ops[1][2]

        def activate(unit):
            raw = final(unit) + bias[col * out_u.shape[0] + unit]
            out_u[unit] = (raw * (1.0 + lax.erf(raw * math.sqrt(0.5))) * 0.5).astype(BF16)

        each(out_u.shape[0], activate)
    for first, second, final, finish, count in all_ops:
        each(count, finish)
    finish_rows()


def in_call(name, number, span, tokens, gain, q_gain, k_gain, weights, up=None):
    own_rows, depth = tokens.shape
    all_rows = own_rows * lax.axis_size("rows")
    cols = lax.axis_size("cols")
    wide = weights[0].shape[1] // cols
    groups = [(3, wide)]
    operands = [tokens, gain[None], q_gain[None], k_gain[None], *weights]
    any_spec, vmem_spec = pl.BlockSpec(memory_space=pl.ANY), pl.BlockSpec(memory_space=pltpu.VMEM)
    in_specs = [vmem_spec] * 4 + [any_spec] * 3
    out_shape = [jax.ShapeDtypeStruct((all_rows, wide), BF16)]
    if up is not None:
        up_bias, up_weight = up
        up_wide = up_tile(up_weight.shape[1] // cols)
        count = up_weight.shape[1] // cols // up_wide
        groups.append((count, up_wide))
        operands += [up_bias.reshape(cols * count, 1, up_wide), up_weight]
        in_specs += [vmem_spec, any_spec]
        out_shape.append(jax.ShapeDtypeStruct((count, all_rows, up_wide), BF16))
    dma = pltpu.SemaphoreType.DMA
    row_count = lax.axis_size("rows")
    scratch = [
        pltpu.VMEM((row_count, own_rows, depth), BF16),
        pltpu.VMEM((4, own_rows, HEAD_DIM), F32),
        dma((3,)),
        dma((3,)),
        dma((row_count,)),
        dma((row_count,)),
        dma((row_count,)),
    ] + [pltpu.VMEM((all_rows, wide), BF16)] * 3
    for count, piece in groups:
        scratch += [
            pltpu.VMEM((count * 4, depth, piece), BF16),
            pltpu.VMEM((2, count, all_rows, piece), BF16),
            pltpu.VMEM((2, count, all_rows, piece), BF16),
            pltpu.VMEM((count, all_rows, piece), BF16),
            pltpu.VMEM((count, all_rows, piece), BF16),
            pltpu.VMEM((count, all_rows, piece), F32),
            dma((count * 4,)),
            dma((2, count)),
            dma((2, count)),
            dma((count,)),
            dma((count,)),
        ]
    return pl.pallas_call(
        functools.partial(in_kernel, span, up is not None, float(depth * cols)),
        name=name,
        out_shape=out_shape,
        in_specs=in_specs,
        out_specs=[vmem_spec] * len(out_shape),
        scratch_shapes=scratch,
        compiler_params=pltpu.CompilerParams(
            collective_id=number, has_side_effects=True, vmem_limit_bytes=VMEM_LIMIT
        ),
    )(*operands)


def out_kernel(has_up, *refs):
    refs = list(refs)
    base, heads, w_out = refs[:3]
    refs = refs[3:]
    if has_up:
        bias, hidden, w_down = refs[:3]
        refs = refs[3:]
    result, accum, right_send, left_send, from_left, from_right = refs[:6]
    r_send, r_recv, l_send, l_recv = refs[6:10]
    groups = [refs[10:18]]
    if has_up:
        groups.append(refs[18:26])
    col, mate, across = places()
    diagonal = mate + across - col
    row, row_count = lax.axis_index("rows"), lax.axis_size("rows")
    own_rows = base.shape[0]
    owners = (col, mate, across, diagonal)
    sources = [(heads, w_out)]
    if has_up:
        sources.append((hidden, w_down))

    def load(group_id, unit, place):
        held, sem = groups[group_id][0], groups[group_id][1]
        source = sources[group_id][1]
        deep = held.shape[1]
        count = held.shape[0] // 4
        start = pl.multiple_of((owners[place] * count + unit) * deep, HEAD_DIM)
        return pltpu.make_async_copy(
            source.at[pl.ds(start, deep)], held.at[place * count + unit], sem.at[place * count + unit]
        )

    for place in range(4):
        for group_id, group in enumerate(groups):
            each(group[0].shape[0] // 4, lambda unit: load(group_id, unit, place).start())
    greet(2)

    def copies(group_id):
        _, _, got, y_send, p_send, f_send, y_recv, p_recv = groups[group_id]
        source = sources[group_id][0]

        def to_across(unit):
            return remote(
                source.at[unit], got.at[1, unit], y_send.at[unit], y_recv.at[unit], {"cols": across}
            )

        def to_mate(unit):
            return remote(
                source.at[unit], got.at[0, unit], p_send.at[unit], p_recv.at[0, unit], {"cols": mate}
            )

        def forward(unit):
            return remote(
                got.at[1, unit], got.at[2, unit], f_send.at[unit], p_recv.at[1, unit], {"cols": mate}
            )

        return to_across, to_mate, forward

    moves = [copies(group_id) for group_id in range(len(groups))]
    for group_id, (to_across, to_mate, forward) in enumerate(moves):
        count = groups[group_id][0].shape[0] // 4
        each(count, lambda unit: to_across(unit).start())
    for group_id, (to_across, to_mate, forward) in enumerate(moves):
        count = groups[group_id][0].shape[0] // 4
        each(count, lambda unit: to_mate(unit).start())
    accum[...] = jnp.zeros_like(accum)

    def add(group_id, unit, place, piece):
        load(group_id, unit, place).wait()
        held = groups[group_id][0]
        count = held.shape[0] // 4
        accum[...] += jnp.dot(piece, held[place * count + unit], preferred_element_type=F32)

    for group_id, (to_across, to_mate, forward) in enumerate(moves):
        count = groups[group_id][0].shape[0] // 4
        source, got = sources[group_id][0], groups[group_id][2]
        each(count, lambda unit: add(group_id, unit, 0, source[unit]))

        def from_mate(unit):
            to_mate(unit).wait_recv()
            add(group_id, unit, 1, got[0, unit])

        each(count, from_mate)

    for group_id, (to_across, to_mate, forward) in enumerate(moves):
        count = groups[group_id][0].shape[0] // 4
        got = groups[group_id][2]

        def from_across(unit):
            to_across(unit).wait_recv()
            forward(unit).start()
            add(group_id, unit, 2, got[1, unit])
            forward(unit).wait_recv()
            add(group_id, unit, 3, got[2, unit])

        each(count, from_across)

    def rows_of(block):
        return accum[pl.ds(pl.multiple_of(block * own_rows, own_rows), own_rows)]

    def to_right(block):
        return remote(
            right_send.at[block], from_left.at[block], r_send.at[block], r_recv.at[block], {"rows": row + 1}
        )

    def to_left(block):
        return remote(
            left_send.at[block], from_right.at[block], l_send.at[block], l_recv.at[block], {"rows": row - 1}
        )

    def run_right(block):
        @pl.when((row < block) & (row == 0))
        def _():
            right_send[block] = rows_of(block).astype(BF16)

        @pl.when((row < block) & (row > 0))
        def _():
            to_right(block).wait_recv()
            right_send[block] = (rows_of(block) + from_left[block].astype(F32)).astype(BF16)

        @pl.when(row < block)
        def _():
            to_right(block).start()

    def run_left(block):
        @pl.when((row > block) & (row == row_count - 1))
        def _():
            left_send[block] = rows_of(block).astype(BF16)

        @pl.when((row > block) & (row < row_count - 1))
        def _():
            to_left(block).wait_recv()
            left_send[block] = (rows_of(block) + from_right[block].astype(F32)).astype(BF16)

        @pl.when(row > block)
        def _():
            to_left(block).start()

    for step in range(row_count - 1):
        run_right(row_count - 1 - step)
        run_left(step)

    for block in range(row_count):

        @pl.when(row == block)
        def _():
            total = rows_of(block)
            if block > 0:
                to_right(block).wait_recv()
                total += from_left[block].astype(F32)
            if block < row_count - 1:
                to_left(block).wait_recv()
                total += from_right[block].astype(F32)
            total += base[...].astype(F32)
            if has_up:
                total += bias[...]
            result[...] = total.astype(BF16)

    for block in range(row_count):

        @pl.when(row < block)
        def _():
            to_right(block).wait_send()

        @pl.when(row > block)
        def _():
            to_left(block).wait_send()

    for group_id, (to_across, to_mate, forward) in enumerate(moves):

        def finish(unit):
            to_across(unit).wait_send()
            to_mate(unit).wait_send()
            forward(unit).wait_send()

        each(groups[group_id][0].shape[0] // 4, finish)


def out_call(name, number, base, heads, w_out, up=None):
    own_rows, width = base.shape
    all_rows, wide = heads.shape
    row_count = lax.axis_size("rows")
    any_spec, vmem_spec = pl.BlockSpec(memory_space=pl.ANY), pl.BlockSpec(memory_space=pltpu.VMEM)
    operands = [base, heads[None], w_out]
    in_specs = [vmem_spec, vmem_spec, any_spec]
    groups = [(1, wide)]
    if up is not None:
        bias, hidden, w_down = up
        operands += [bias[None], hidden, w_down]
        in_specs += [vmem_spec, vmem_spec, any_spec]
        groups.append((hidden.shape[0], hidden.shape[2]))
    dma = pltpu.SemaphoreType.DMA
    block = pltpu.VMEM((row_count, own_rows, width), BF16)
    scratch = [pltpu.VMEM((all_rows, width), F32)] + [block] * 4 + [dma((row_count,))] * 4
    for count, piece in groups:
        scratch += [
            pltpu.VMEM((4 * count, piece, width), BF16),
            dma((4 * count,)),
            pltpu.VMEM((3, count, all_rows, piece), BF16),
            dma((count,)),
            dma((count,)),
            dma((count,)),
            dma((count,)),
            dma((2, count)),
        ]
    return pl.pallas_call(
        functools.partial(out_kernel, up is not None),
        name=name,
        out_shape=jax.ShapeDtypeStruct((own_rows, width), BF16),
        in_specs=in_specs,
        out_specs=vmem_spec,
        scratch_shapes=scratch,
        compiler_params=pltpu.CompilerParams(
            collective_id=number, has_side_effects=True, vmem_limit_bytes=VMEM_LIMIT
        ),
    )(*operands)


def up_tile(columns):
    for tile in (4 * HEAD_DIM, 2 * HEAD_DIM, HEAD_DIM):
        if columns % tile == 0:
            return tile
    return columns


def kernel_body(
    camera_tokens,
    norm_gain,
    query_weight,
    key_weight,
    value_weight,
    query_gain,
    key_gain,
    out_weight,
    up_weight,
    up_bias,
    down_weight,
    down_bias,
    join_gain,
    join_query,
    join_key,
    join_value,
    join_query_gain,
    join_key_gain,
    join_out,
):
    all_rows = camera_tokens.shape[0] * lax.axis_size("rows")
    heads, hidden = in_call(
        "camera_in",
        0,
        TOK_CAM,
        camera_tokens,
        norm_gain,
        query_gain,
        key_gain,
        (query_weight, key_weight, value_weight),
        (up_bias, up_weight),
    )
    layer_own = out_call(
        "camera_out", 1, camera_tokens, heads, out_weight, (down_bias, hidden, down_weight)
    )
    (joined,) = in_call(
        "join_in",
        2,
        all_rows,
        layer_own,
        join_gain,
        join_query_gain,
        join_key_gain,
        (join_query, join_key, join_value),
    )
    return out_call("join_out", 3, layer_own, joined, join_out)


def fits(mesh):
    cols, rows = mesh.shape["cols"], mesh.shape["rows"]
    return cols == 4 and rows > 1 and D % (rows * cols * HEAD_DIM) == 0


def solution(mesh):
    in_specs = (
        P(("groups", "rows"), "cols"),
        P("cols"),
        P("cols", "rows"),
        P("cols", "rows"),
        P("cols", "rows"),
        P("rows"),
        P("rows"),
        P("rows", "cols"),
        P("cols", "rows"),
        P("rows"),
        P("rows", "cols"),
        P("cols"),
        P("cols"),
        P("cols", "rows"),
        P("cols", "rows"),
        P("cols", "rows"),
        P("rows"),
        P("rows"),
        P("rows", "cols"),
    )
    out_specs = P(("groups", "rows"), "cols")
    body = kernel_body if fits(mesh) else plain_body
    return jax.shard_map(body, mesh=mesh, in_specs=in_specs, out_specs=out_specs, check_vma=False)
```

```python
import functools
import math

import jax
import jax.numpy as jnp
from jax import lax
from jax.experimental import pallas as pl
from jax.experimental.pallas import tpu as pltpu
from jax.sharding import PartitionSpec as P

HEAD_DIM = 128
TOK_CAM = 64
D = 6144


EPS = 1e-06


def partner_2(array, axis, bit):
    return lax.ppermute(array, axis, [(i, i ^ 1 << bit) for i in range(lax.axis_size(axis))])


def normalize(values, scales, moments):
    row_mean = moments[0] / D
    row_var = moments[1] / D - row_mean * row_mean
    return ((values - row_mean[:, None]) * lax.rsqrt(row_var[:, None] + EPS) * scales).astype(
        jnp.bfloat16
    )


def shard_moments(values):
    return lax.psum((jnp.sum(values, 1), jnp.sum(values * values, 1)), "cols")


def head_norm(values, scales):
    row_count = values.shape[0]
    grouped = values.reshape(row_count, -1, HEAD_DIM)
    row_mean = jnp.mean(grouped, -1, keepdims=True)
    row_var = jnp.mean(grouped * grouped, -1, keepdims=True) - row_mean * row_mean
    normed = (grouped - row_mean) * lax.rsqrt(row_var + EPS)
    return (normed.reshape(row_count, -1) * scales).astype(jnp.bfloat16)


def attend(queries, key_rows, val_rows):
    inv_root = 1.0 / math.sqrt(HEAD_DIM)
    scores = (
        jnp.einsum("bqhd,bkhd->bhqk", queries, key_rows, preferred_element_type=jnp.float32)
        * inv_root
    )
    row_max = jnp.max(scores, -1, keepdims=True)
    weights = jnp.exp(scores - row_max)
    row_sum = jnp.sum(weights, -1)
    blended = jnp.einsum(
        "bhqk,bkhd->bqhd",
        weights.astype(jnp.bfloat16),
        val_rows,
        preferred_element_type=jnp.float32,
    )
    return blended / jnp.transpose(row_sum, (0, 2, 1))[..., None]


def to_heads(matrix, blocks):
    return matrix.reshape(blocks, -1, matrix.shape[1] // HEAD_DIM, HEAD_DIM)


def camera_attention(queries, key_rows, val_rows):
    local_rows = queries.shape[0]
    if local_rows >= TOK_CAM:
        blocks = local_rows // TOK_CAM
        result = attend(
            to_heads(queries, blocks), to_heads(key_rows, blocks), to_heads(val_rows, blocks)
        )
    else:
        cam_span = TOK_CAM // local_rows
        position = lax.axis_index("cols")
        key_value = jnp.stack((key_rows, val_rows))
        for which_bit in range(cam_span.bit_length() - 1):
            partner = partner_2(key_value, "cols", which_bit)
            is_lower = position >> which_bit & 1 == 0
            key_value = jnp.where(
                is_lower,
                jnp.concatenate((key_value, partner), 1),
                jnp.concatenate((partner, key_value), 1),
            )
        result = attend(to_heads(queries, 1), to_heads(key_value[0], 1), to_heads(key_value[1], 1))
    return result.reshape(local_rows, -1).astype(jnp.bfloat16)


def plain_body(
    camera_tokens,
    norm_gain,
    query_weight,
    key_weight,
    value_weight,
    query_gain,
    key_gain,
    out_weight,
    up_weight,
    up_bias,
    down_weight,
    down_bias,
    join_gain,
    join_query,
    join_key,
    join_value,
    join_query_gain,
    join_key_gain,
    join_out,
):
    own_rows = camera_tokens.shape[0]
    all_rows = own_rows * lax.axis_size("rows")
    col_rows = all_rows // lax.axis_size("cols")
    attn_width = query_weight.shape[1]
    start_f32 = camera_tokens.astype(jnp.float32)
    normed_all = lax.all_gather(
        normalize(start_f32, norm_gain, shard_moments(start_f32)), "rows", axis=0, tiled=True
    )
    joint_weight = jnp.concatenate((query_weight, key_weight, value_weight, up_weight), 1)
    joint = lax.psum_scatter(
        jnp.dot(normed_all, joint_weight, preferred_element_type=jnp.float32),
        "cols",
        scatter_dimension=0,
        tiled=True,
    )
    up_sum = joint[:, 3 * attn_width :]
    hidden = jax.nn.gelu(up_sum + up_bias, approximate=False).astype(jnp.bfloat16)
    attended = camera_attention(
        head_norm(joint[:, :attn_width], query_gain),
        head_norm(joint[:, attn_width : 2 * attn_width], key_gain),
        joint[:, 2 * attn_width : 3 * attn_width].astype(jnp.bfloat16),
    )
    attn_all, hidden_all = (
        lax.all_gather(attended, "cols", axis=0, tiled=True),
        lax.all_gather(hidden, "cols", axis=0, tiled=True),
    )
    mixed = lax.psum_scatter(
        jnp.dot(attn_all, out_weight, preferred_element_type=jnp.float32)
        + jnp.dot(hidden_all, down_weight, preferred_element_type=jnp.float32),
        "rows",
        scatter_dimension=0,
        tiled=True,
    )
    layer_own = (start_f32 + mixed + down_bias).astype(jnp.bfloat16)
    layer_f32 = layer_own.astype(jnp.float32)
    join_in = lax.all_gather(
        normalize(layer_f32, join_gain, shard_moments(layer_f32)), "rows", axis=0, tiled=True
    )
    join_weight = jnp.concatenate((join_query, join_key, join_value), 1)
    join_joint = lax.psum_scatter(
        jnp.dot(join_in, join_weight, preferred_element_type=jnp.float32),
        "cols",
        scatter_dimension=0,
        tiled=True,
    )
    join_q = head_norm(join_joint[:, :attn_width], join_query_gain)
    join_k = head_norm(join_joint[:, attn_width : 2 * attn_width], join_key_gain)
    join_v = join_joint[:, 2 * attn_width :].astype(jnp.bfloat16)
    heads_here = attn_width // HEAD_DIM
    query_heads = join_q.reshape(col_rows, heads_here, HEAD_DIM)
    inv_root = 1.0 / math.sqrt(HEAD_DIM)
    run_max = jnp.full((heads_here, col_rows), -jnp.inf, jnp.float32)
    run_sum = jnp.zeros((heads_here, col_rows), jnp.float32)
    accum = jnp.zeros((col_rows, heads_here, HEAD_DIM), jnp.float32)
    key_part = lax.all_gather(join_k, "cols", axis=0, tiled=True)
    val_part = lax.all_gather(join_v, "cols", axis=0, tiled=True)
    row_count = key_part.shape[0]
    key_heads = key_part.reshape(row_count, heads_here, HEAD_DIM)
    val_heads = val_part.reshape(row_count, heads_here, HEAD_DIM)
    scores = (
        jnp.einsum("qhd,khd->hqk", query_heads, key_heads, preferred_element_type=jnp.float32)
        * inv_root
    )
    new_max = jnp.max(scores, -1)
    factor = jnp.exp(run_max - new_max)
    weights = jnp.exp(scores - new_max[..., None])
    run_sum = run_sum * factor + jnp.sum(weights, -1)
    accum = accum * jnp.transpose(factor)[..., None] + jnp.einsum(
        "hqk,khd->qhd", weights.astype(jnp.bfloat16), val_heads, preferred_element_type=jnp.float32
    )
    run_max, run_sum, accum = (new_max, run_sum, accum)
    joined_attn = (
        (accum / jnp.transpose(run_sum)[..., None])
        .reshape(col_rows, attn_width)
        .astype(jnp.bfloat16)
    )
    joined_all = lax.all_gather(joined_attn, "cols", axis=0, tiled=True)
    result = lax.psum_scatter(
        jnp.dot(joined_all, join_out, preferred_element_type=jnp.float32),
        "rows",
        scatter_dimension=0,
        tiled=True,
    )
    return (layer_own.astype(jnp.float32) + result).astype(jnp.bfloat16)


F32 = jnp.float32
BF16 = jnp.bfloat16
MESH = pl.DeviceIdType.MESH
VMEM_LIMIT = 66 * 1024 * 1024 - 3 * 1024 * 1024


def each(count, step):
    lax.fori_loop(0, count, lambda i, carry: (step(i), carry)[1], None)


def remote(src, dst, send, recv, device):
    return pltpu.make_async_remote_copy(
        src_ref=src,
        dst_ref=dst,
        send_sem=send,
        recv_sem=recv,
        device_id=device,
        device_id_type=MESH,
    )


def places():
    col = lax.axis_index("cols")
    core = lax.rem(col, 2)
    return col, col + 1 - 2 * core, lax.rem(col + 2, 4)


def greet(cols_away):
    col, row, row_count = lax.axis_index("cols"), lax.axis_index("rows"), lax.axis_size("rows")
    barrier = pltpu.get_barrier_semaphore()
    _, mate, across = places()
    others = {1: mate, 2: across}
    if cols_away == 3:
        others[3] = mate + across - col
    for other in others.values():
        pl.semaphore_signal(barrier, inc=1, device_id={"cols": other}, device_id_type=MESH)

    @pl.when(row > 0)
    def _():
        pl.semaphore_signal(barrier, inc=1, device_id={"rows": row - 1}, device_id_type=MESH)

    @pl.when(row < row_count - 1)
    def _():
        pl.semaphore_signal(barrier, inc=1, device_id={"rows": row + 1}, device_id_type=MESH)

    inner = (row > 0) & (row < row_count - 1)

    @pl.when(inner)
    def _():
        pl.semaphore_wait(barrier, len(others) + 2)

    @pl.when(jnp.logical_not(inner))
    def _():
        pl.semaphore_wait(barrier, len(others) + 1)


def gather_rows(normed, send_r, send_l, arrive):
    row, row_count = lax.axis_index("rows"), lax.axis_size("rows")

    def to_right(block):
        return remote(
            normed.at[block], normed.at[block], send_r.at[block], arrive.at[block], {"rows": row + 1}
        )

    def to_left(block):
        return remote(
            normed.at[block], normed.at[block], send_l.at[block], arrive.at[block], {"rows": row - 1}
        )

    def pass_on(from_left, block):
        if from_left:

            @pl.when(row < row_count - 1)
            def _():
                to_right(block).start()
        else:

            @pl.when(row > 0)
            def _():
                to_left(block).start()

    pass_on(True, row)
    pass_on(False, row)

    def take(away):
        @pl.when(row >= away)
        def _():
            to_right(row - away).wait_recv()
            pass_on(True, row - away)

        @pl.when(row + away < row_count)
        def _():
            to_left(row + away).wait_recv()
            pass_on(False, row + away)

    def finish():
        for block in range(row_count):

            @pl.when((row >= block) & (row < row_count - 1))
            def _():
                to_right(block).wait_send()

            @pl.when((row <= block) & (row > 0))
            def _():
                to_left(block).wait_send()

    return take, finish


def norm_heads(values, scales):
    parts = []
    for start in range(0, values.shape[1], HEAD_DIM):
        part = values[:, start : start + HEAD_DIM]
        mean = jnp.mean(part, -1, keepdims=True)
        var = jnp.mean(part * part, -1, keepdims=True) - mean * mean
        parts.append((part - mean) * lax.rsqrt(var + EPS))
    return (jnp.concatenate(parts, 1) * scales).astype(BF16)


def soft_blend(query, keys, values):
    scores = lax.dot_general(
        query, keys, (((1,), (1,)), ((), ())), preferred_element_type=F32
    ) * (1.0 / math.sqrt(HEAD_DIM))
    weights = jnp.exp(scores - jnp.max(scores, -1, keepdims=True))
    total = jnp.sum(weights, -1, keepdims=True)
    blended = jnp.dot(weights.astype(BF16), values, preferred_element_type=F32)
    return (blended / total).astype(BF16)


def in_kernel(span, has_up, width, *refs):
    refs = list(refs)
    tokens, gain, q_gain, k_gain, wq, wk, wv = refs[:7]
    refs = refs[7:]
    if has_up:
        bias, w_up = refs[:2]
        refs = refs[2:]
    out_a = refs.pop(0)
    if has_up:
        out_u = refs.pop(0)
    normed, moments, m_send, m_recv, z_right, z_left, z_arrive, queries, keys, values = refs[:10]
    groups = [refs[10:21]]
    if has_up:
        groups.append(refs[21:32])
    col, mate, across = places()
    diagonal = mate + across - col
    row, row_count = lax.axis_index("rows"), lax.axis_size("rows")
    own_rows = tokens.shape[0]
    near = row_count // 2

    def load(group, unit, owner, source, start):
        held = group[0]
        columns = pl.ds(pl.multiple_of(start, HEAD_DIM), held.shape[-1])
        return pltpu.make_async_copy(
            source.at[:, columns], held.at[unit * 4 + owner], group[6].at[unit * 4 + owner]
        )

    def loads(group_id, unit, owner, which=None):
        group = groups[group_id]
        wide = group[0].shape[-1]
        if group_id == 0:
            return load(group, unit, owner, (wq, wk, wv)[which], owner * wide)
        return load(group, unit, owner, w_up, owner * (groups[1][5].shape[0] * wide) + unit * wide)

    def start_loads(owner):
        for which in range(3):
            loads(0, which, owner, which).start()
        if has_up:
            each(groups[1][5].shape[0], lambda unit: loads(1, unit, owner).start())

    order = (diagonal, across, mate, col)
    for owner in order:
        start_loads(owner)
    greet(3)

    own = tokens[...].astype(F32)
    lane = lax.broadcasted_iota(jnp.int32, (own_rows, HEAD_DIM), 1)
    mine = jnp.where(
        lane < HEAD_DIM // 2,
        jnp.sum(own, 1, keepdims=True),
        jnp.sum(own * own, 1, keepdims=True),
    )
    moments[3] = mine
    swaps = []
    for slot, other in enumerate((mate, across, diagonal)):
        swap = remote(
            moments.at[3], moments.at[slot], m_send.at[slot], m_recv.at[slot], {"cols": other}
        )
        swap.start()
        swaps.append(swap)
    for swap in swaps:
        swap.wait_recv()
    total = (moments[3] + moments[0]) + (moments[1] + moments[2])
    mean = total[:, :1] / width
    var = total[:, HEAD_DIM // 2 : HEAD_DIM // 2 + 1] / width - mean * mean
    normed[row] = ((own - mean) * lax.rsqrt(var + EPS) * gain[...].reshape(1, -1)).astype(BF16)
    take_rows, finish_rows = gather_rows(normed, z_right, z_left, z_arrive)
    for swap in swaps:
        swap.wait_send()

    def ops(group):
        held, p_send, p_recv, y_send, y_recv, own_sum, _, ps, pr, ys, yr = group

        def product(unit, half, owner, fresh):
            weight = held.at[unit * 4 + owner]
            if fresh:
                pltpu.make_async_copy(weight, weight, group[6].at[unit * 4 + owner]).wait()
            left = normed[pl.ds(half * near, near)].reshape(near * own_rows, normed.shape[-1])
            return jnp.dot(left, weight[...], preferred_element_type=F32)

        def to_mate(kind, unit, half):
            return remote(
                p_send.at[kind, unit, half],
                p_recv.at[kind, unit, half],
                ps.at[kind, unit, half],
                pr.at[kind, unit, half],
                {"cols": mate},
            )

        def to_across(unit, half):
            return remote(
                y_send.at[unit, half],
                y_recv.at[unit, half],
                ys.at[unit, half],
                yr.at[unit, half],
                {"cols": across},
            )

        def first(unit, half, fresh):
            p_send[0, unit, half] = product(unit, half, diagonal, fresh).astype(BF16)
            to_mate(0, unit, half).start()
            partial = product(unit, half, across, fresh)
            to_mate(0, unit, half).wait_recv()
            y_send[unit, half] = (partial + p_recv[0, unit, half].astype(F32)).astype(BF16)
            to_across(unit, half).start()

        def second(unit, half, fresh):
            p_send[1, unit, half] = product(unit, half, mate, fresh).astype(BF16)
            to_mate(1, unit, half).start()
            partial = product(unit, half, col, fresh)
            to_mate(1, unit, half).wait_recv()
            own_sum[unit, half] = partial + p_recv[1, unit, half].astype(F32)

        def final(unit, half):
            to_across(unit, half).wait_recv()
            return own_sum[unit, half] + y_recv[unit, half].astype(F32)

        def finish(unit):
            for half in range(2):
                to_mate(0, unit, half).wait_send()
                to_mate(1, unit, half).wait_send()
                to_across(unit, half).wait_send()

        return first, second, final, finish, own_sum.shape[0]

    all_ops = [ops(group) for group in groups]
    for away in range(1, near):
        take_rows(away)
    home = row // near
    for half, fresh in ((home, True), (1 - home, False)):
        for first, second, final, finish, count in all_ops:
            each(count, lambda unit: first(unit, half, fresh))
        if fresh:
            for away in range(near, row_count - 1):
                take_rows(away)
        for first, second, final, finish, count in all_ops:
            each(count, lambda unit: second(unit, half, fresh))
        if fresh:
            take_rows(row_count - 1)
    final = all_ops[0][2]
    wide = groups[0][0].shape[-1]
    mine = pl.ds(pl.multiple_of(col * wide, HEAD_DIM), wide)
    half_rows = near * own_rows
    for half in range(2):
        rows = slice(half * half_rows, (half + 1) * half_rows)
        queries[rows] = norm_heads(final(0, half), q_gain[mine].reshape(1, -1))
        keys[rows] = norm_heads(final(1, half), k_gain[mine].reshape(1, -1))
        values[rows] = final(2, half).astype(BF16)

    def camera(which):
        rows = pl.ds(pl.multiple_of(which * span, span), span)
        local = pl.ds(pl.multiple_of(lax.rem(which * span, half_rows), span), span)
        for start in range(0, wide, HEAD_DIM):
            head = slice(start, start + HEAD_DIM)
            out_a[which * span // half_rows, local, head] = soft_blend(
                queries[rows, head], keys[rows, head], values[rows, head]
            )

    def joint(half):
        for start in range(0, wide, HEAD_DIM):
            head = slice(start, start + HEAD_DIM)
            rows = pl.ds(pl.multiple_of(half * half_rows, half_rows), half_rows)
            out_a[half, :, head] = soft_blend(queries[rows, head], keys[:, head], values[:, head])

    if span == 2 * half_rows:
        each(2, joint)
    else:
        each(2 * half_rows // span, camera)
    if has_up:
        final = all_ops[1][2]

        def activate(unit):
            for half in range(2):
                raw = final(unit, half) + bias[col * out_u.shape[0] + unit]
                out_u[unit, half] = (raw * (1.0 + lax.erf(raw * math.sqrt(0.5))) * 0.5).astype(BF16)

        each(out_u.shape[0], activate)
    for first, second, final, finish, count in all_ops:
        each(count, finish)
    finish_rows()


def in_call(name, number, span, tokens, gain, q_gain, k_gain, weights, up=None):
    own_rows, depth = tokens.shape
    all_rows = own_rows * lax.axis_size("rows")
    cols = lax.axis_size("cols")
    wide = weights[0].shape[1] // cols
    groups = [(3, wide)]
    operands = [tokens, gain, q_gain, k_gain, *weights]
    any_spec, vmem_spec = pl.BlockSpec(memory_space=pl.ANY), pl.BlockSpec(memory_space=pltpu.VMEM)
    in_specs = [vmem_spec] * 4 + [any_spec] * 3
    half_rows = all_rows // 2
    out_shape = [jax.ShapeDtypeStruct((2, half_rows, wide), BF16)]
    if up is not None:
        up_bias, up_weight = up
        up_wide = up_tile(up_weight.shape[1] // cols)
        count = up_weight.shape[1] // cols // up_wide
        groups.append((count, up_wide))
        operands += [up_bias.reshape(cols * count, 1, up_wide), up_weight]
        in_specs += [vmem_spec, any_spec]
        out_shape.append(jax.ShapeDtypeStruct((count, 2, half_rows, up_wide), BF16))
    dma = pltpu.SemaphoreType.DMA
    row_count = lax.axis_size("rows")
    scratch = [
        pltpu.VMEM((row_count, own_rows, depth), BF16),
        pltpu.VMEM((4, own_rows, HEAD_DIM), F32),
        dma((3,)),
        dma((3,)),
        dma((row_count,)),
        dma((row_count,)),
        dma((row_count,)),
    ] + [pltpu.VMEM((all_rows, wide), BF16)] * 3
    for count, piece in groups:
        scratch += [
            pltpu.VMEM((count * 4, depth, piece), BF16),
            pltpu.VMEM((2, count, 2, half_rows, piece), BF16),
            pltpu.VMEM((2, count, 2, half_rows, piece), BF16),
            pltpu.VMEM((count, 2, half_rows, piece), BF16),
            pltpu.VMEM((count, 2, half_rows, piece), BF16),
            pltpu.VMEM((count, 2, half_rows, piece), F32),
            dma((count * 4,)),
            dma((2, count, 2)),
            dma((2, count, 2)),
            dma((count, 2)),
            dma((count, 2)),
        ]
    return pl.pallas_call(
        functools.partial(in_kernel, span, up is not None, float(depth * cols)),
        name=name,
        out_shape=out_shape,
        in_specs=in_specs,
        out_specs=[vmem_spec] * len(out_shape),
        scratch_shapes=scratch,
        compiler_params=pltpu.CompilerParams(
            collective_id=number, has_side_effects=True, vmem_limit_bytes=VMEM_LIMIT
        ),
    )(*operands)


def out_kernel(has_up, *refs):
    refs = list(refs)
    base, heads, w_out = refs[:3]
    refs = refs[3:]
    if has_up:
        bias, hidden, w_down = refs[:3]
        refs = refs[3:]
    result, accum, right_send, left_send, from_left, from_right = refs[:6]
    r_send, r_recv, l_send, l_recv = refs[6:10]
    groups = [refs[10:18]]
    if has_up:
        groups.append(refs[18:26])
    col, mate, across = places()
    diagonal = mate + across - col
    row, row_count = lax.axis_index("rows"), lax.axis_size("rows")
    own_rows = base.shape[0]
    near = row_count // 2
    owners = (col, mate, across, diagonal)
    sources = [(heads, w_out)]
    if has_up:
        sources.append((hidden, w_down))

    def load(group_id, unit, place):
        held, sem = groups[group_id][0], groups[group_id][1]
        source = sources[group_id][1]
        deep = held.shape[1]
        count = held.shape[0] // 4
        start = pl.multiple_of((owners[place] * count + unit) * deep, HEAD_DIM)
        return pltpu.make_async_copy(
            source.at[pl.ds(start, deep)], held.at[place * count + unit], sem.at[place * count + unit]
        )

    for place in range(4):
        for group_id, group in enumerate(groups):
            each(group[0].shape[0] // 4, lambda unit: load(group_id, unit, place).start())
    greet(2)

    def copies(group_id):
        _, _, got, y_send, p_send, f_send, y_recv, p_recv = groups[group_id]
        source = sources[group_id][0]

        def to_across(unit, half):
            return remote(
                source.at[unit, half],
                got.at[1, unit, half],
                y_send.at[unit, half],
                y_recv.at[unit, half],
                {"cols": across},
            )

        def to_mate(unit, half):
            return remote(
                source.at[unit, half],
                got.at[0, unit, half],
                p_send.at[unit, half],
                p_recv.at[0, unit, half],
                {"cols": mate},
            )

        def forward(unit, half):
            return remote(
                got.at[1, unit, half],
                got.at[2, unit, half],
                f_send.at[unit, half],
                p_recv.at[1, unit, half],
                {"cols": mate},
            )

        return to_across, to_mate, forward, groups[group_id][0].shape[0] // 4

    moves = [copies(group_id) for group_id in range(len(groups))]
    home = row // near
    halves = ((1 - home, True), (home, False))
    for half, _ in halves:
        for to_across, to_mate, forward, count in moves:
            each(count, lambda unit: to_across(unit, half).start())
            each(count, lambda unit: to_mate(unit, half).start())

    def add(group_id, unit, place, half, fresh, piece, begin=False):
        if fresh:
            load(group_id, unit, place).wait()
        held = groups[group_id][0]
        count = held.shape[0] // 4
        part = jnp.dot(piece, held[place * count + unit], preferred_element_type=F32)
        if begin:
            accum[half] = part
        else:
            accum[half] += part

    def near_chunks(half, fresh):
        for group_id, (to_across, to_mate, forward, count) in enumerate(moves):
            source, got = sources[group_id][0], groups[group_id][2]
            if group_id == 0:
                add(0, 0, 0, half, fresh, source[0, half], True)
            else:
                each(count, lambda unit: add(group_id, unit, 0, half, fresh, source[unit, half]))

            def from_mate(unit):
                to_mate(unit, half).wait_recv()
                add(group_id, unit, 1, half, fresh, got[0, unit, half])

            each(count, from_mate)

    def far_chunks(half, fresh):
        for group_id, (to_across, to_mate, forward, count) in enumerate(moves):
            got = groups[group_id][2]

            def from_across(unit):
                to_across(unit, half).wait_recv()
                forward(unit, half).start()
                add(group_id, unit, 2, half, fresh, got[1, unit, half])
                forward(unit, half).wait_recv()
                add(group_id, unit, 3, half, fresh, got[2, unit, half])

            each(count, from_across)

    def rows_of(block):
        return accum[block // near, (block % near) * own_rows : (block % near + 1) * own_rows]

    def to_right(block):
        return remote(
            right_send.at[block], from_left.at[block], r_send.at[block], r_recv.at[block], {"rows": row + 1}
        )

    def to_left(block):
        return remote(
            left_send.at[block], from_right.at[block], l_send.at[block], l_recv.at[block], {"rows": row - 1}
        )

    def run_right(block):
        @pl.when((row < block) & (row == 0))
        def _():
            right_send[block] = rows_of(block).astype(BF16)

        @pl.when((row < block) & (row > 0))
        def _():
            to_right(block).wait_recv()
            right_send[block] = (rows_of(block) + from_left[block].astype(F32)).astype(BF16)

        @pl.when(row < block)
        def _():
            to_right(block).start()

    def run_left(block):
        @pl.when((row > block) & (row == row_count - 1))
        def _():
            left_send[block] = rows_of(block).astype(BF16)

        @pl.when((row > block) & (row < row_count - 1))
        def _():
            to_left(block).wait_recv()
            left_send[block] = (rows_of(block) + from_right[block].astype(F32)).astype(BF16)

        @pl.when(row > block)
        def _():
            to_left(block).start()

    def send_far(from_end):
        at_end = (row == 0) | (row == row_count - 1)
        now = at_end if from_end else jnp.logical_not(at_end)
        for step in range(near):

            @pl.when(now & (row < near))
            def _():
                run_right(row_count - 1 - step)

            @pl.when(now & (row >= near))
            def _():
                run_left(step)

    near_chunks(*halves[0])
    far_chunks(*halves[0])
    send_far(True)
    near_chunks(*halves[1])
    send_far(False)
    far_chunks(*halves[1])
    for step in range(row_count - 1):
        block = row_count - 1 - step

        @pl.when(home == block // near)
        def _():
            run_right(block)

    for block in range(row_count - 1):

        @pl.when(home == block // near)
        def _():
            run_left(block)

    for block in range(row_count):

        @pl.when(row == block)
        def _():
            total = rows_of(block)
            if block > 0:
                to_right(block).wait_recv()
                total += from_left[block].astype(F32)
            if block < row_count - 1:
                to_left(block).wait_recv()
                total += from_right[block].astype(F32)
            total += base[...].astype(F32)
            if has_up:
                total += bias[...].reshape(1, -1)
            result[...] = total.astype(BF16)

    for block in range(row_count):

        @pl.when(row < block)
        def _():
            to_right(block).wait_send()

        @pl.when(row > block)
        def _():
            to_left(block).wait_send()

    for to_across, to_mate, forward, count in moves:

        def finish(unit):
            for half in range(2):
                to_across(unit, half).wait_send()
                to_mate(unit, half).wait_send()
                forward(unit, half).wait_send()

        each(count, finish)


def out_call(name, number, base, heads, w_out, up=None):
    own_rows, width = base.shape
    _, half_rows, wide = heads.shape
    row_count = lax.axis_size("rows")
    any_spec, vmem_spec = pl.BlockSpec(memory_space=pl.ANY), pl.BlockSpec(memory_space=pltpu.VMEM)
    operands = [base, heads[None], w_out]
    in_specs = [vmem_spec, vmem_spec, any_spec]
    groups = [(1, wide)]
    if up is not None:
        bias, hidden, w_down = up
        operands += [bias, hidden, w_down]
        in_specs += [vmem_spec, vmem_spec, any_spec]
        groups.append((hidden.shape[0], hidden.shape[3]))
    dma = pltpu.SemaphoreType.DMA
    block = pltpu.VMEM((row_count, own_rows, width), BF16)
    scratch = [pltpu.VMEM((2, half_rows, width), F32)] + [block] * 4 + [dma((row_count,))] * 4
    for count, piece in groups:
        scratch += [
            pltpu.VMEM((4 * count, piece, width), BF16),
            dma((4 * count,)),
            pltpu.VMEM((3, count, 2, half_rows, piece), BF16),
            dma((count, 2)),
            dma((count, 2)),
            dma((count, 2)),
            dma((count, 2)),
            dma((2, count, 2)),
        ]
    return pl.pallas_call(
        functools.partial(out_kernel, up is not None),
        name=name,
        out_shape=jax.ShapeDtypeStruct((own_rows, width), BF16),
        in_specs=in_specs,
        out_specs=vmem_spec,
        scratch_shapes=scratch,
        compiler_params=pltpu.CompilerParams(
            collective_id=number, has_side_effects=True, vmem_limit_bytes=VMEM_LIMIT
        ),
    )(*operands)


def up_tile(columns):
    for tile in (4 * HEAD_DIM, 2 * HEAD_DIM, HEAD_DIM):
        if columns % tile == 0:
            return tile
    return columns


def kernel_body(
    camera_tokens,
    norm_gain,
    query_weight,
    key_weight,
    value_weight,
    query_gain,
    key_gain,
    out_weight,
    up_weight,
    up_bias,
    down_weight,
    down_bias,
    join_gain,
    join_query,
    join_key,
    join_value,
    join_query_gain,
    join_key_gain,
    join_out,
):
    all_rows = camera_tokens.shape[0] * lax.axis_size("rows")
    heads, hidden = in_call(
        "camera_in",
        0,
        TOK_CAM,
        camera_tokens,
        norm_gain,
        query_gain,
        key_gain,
        (query_weight, key_weight, value_weight),
        (up_bias, up_weight),
    )
    layer_own = out_call(
        "camera_out", 1, camera_tokens, heads, out_weight, (down_bias, hidden, down_weight)
    )
    (joined,) = in_call(
        "join_in",
        2,
        all_rows,
        layer_own,
        join_gain,
        join_query_gain,
        join_key_gain,
        (join_query, join_key, join_value),
    )
    return out_call("join_out", 3, layer_own, joined, join_out)


def fits(mesh):
    cols, rows = mesh.shape["cols"], mesh.shape["rows"]
    return cols == 4 and rows > 2 and rows % 2 == 0 and D % (rows * cols * HEAD_DIM) == 0


def solution(mesh):
    in_specs = (
        P(("groups", "rows"), "cols"),
        P("cols"),
        P("cols", "rows"),
        P("cols", "rows"),
        P("cols", "rows"),
        P("rows"),
        P("rows"),
        P("rows", "cols"),
        P("cols", "rows"),
        P("rows"),
        P("rows", "cols"),
        P("cols"),
        P("cols"),
        P("cols", "rows"),
        P("cols", "rows"),
        P("cols", "rows"),
        P("rows"),
        P("rows"),
        P("rows", "cols"),
    )
    out_specs = P(("groups", "rows"), "cols")
    body = kernel_body if fits(mesh) else plain_body
    return jax.shard_map(body, mesh=mesh, in_specs=in_specs, out_specs=out_specs, check_vma=False)
```

```python
import functools
import math

import jax
import jax.numpy as jnp
from jax import lax
from jax.experimental import pallas as pl
from jax.experimental.pallas import tpu as pltpu
from jax.sharding import PartitionSpec as P

HEAD_DIM = 128
TOK_CAM = 64
D = 6144


EPS = 1e-06


def partner_2(array, axis, bit):
    return lax.ppermute(array, axis, [(i, i ^ 1 << bit) for i in range(lax.axis_size(axis))])


def normalize(values, scales, moments):
    row_mean = moments[0] / D
    row_var = moments[1] / D - row_mean * row_mean
    return ((values - row_mean[:, None]) * lax.rsqrt(row_var[:, None] + EPS) * scales).astype(
        jnp.bfloat16
    )


def shard_moments(values):
    return lax.psum((jnp.sum(values, 1), jnp.sum(values * values, 1)), "cols")


def head_norm(values, scales):
    row_count = values.shape[0]
    grouped = values.reshape(row_count, -1, HEAD_DIM)
    row_mean = jnp.mean(grouped, -1, keepdims=True)
    row_var = jnp.mean(grouped * grouped, -1, keepdims=True) - row_mean * row_mean
    normed = (grouped - row_mean) * lax.rsqrt(row_var + EPS)
    return (normed.reshape(row_count, -1) * scales).astype(jnp.bfloat16)


def attend(queries, key_rows, val_rows):
    inv_root = 1.0 / math.sqrt(HEAD_DIM)
    scores = (
        jnp.einsum("bqhd,bkhd->bhqk", queries, key_rows, preferred_element_type=jnp.float32)
        * inv_root
    )
    row_max = jnp.max(scores, -1, keepdims=True)
    weights = jnp.exp(scores - row_max)
    row_sum = jnp.sum(weights, -1)
    blended = jnp.einsum(
        "bhqk,bkhd->bqhd",
        weights.astype(jnp.bfloat16),
        val_rows,
        preferred_element_type=jnp.float32,
    )
    return blended / jnp.transpose(row_sum, (0, 2, 1))[..., None]


def to_heads(matrix, blocks):
    return matrix.reshape(blocks, -1, matrix.shape[1] // HEAD_DIM, HEAD_DIM)


def camera_attention(queries, key_rows, val_rows):
    local_rows = queries.shape[0]
    if local_rows >= TOK_CAM:
        blocks = local_rows // TOK_CAM
        result = attend(
            to_heads(queries, blocks), to_heads(key_rows, blocks), to_heads(val_rows, blocks)
        )
    else:
        cam_span = TOK_CAM // local_rows
        position = lax.axis_index("cols")
        key_value = jnp.stack((key_rows, val_rows))
        for which_bit in range(cam_span.bit_length() - 1):
            partner = partner_2(key_value, "cols", which_bit)
            is_lower = position >> which_bit & 1 == 0
            key_value = jnp.where(
                is_lower,
                jnp.concatenate((key_value, partner), 1),
                jnp.concatenate((partner, key_value), 1),
            )
        result = attend(to_heads(queries, 1), to_heads(key_value[0], 1), to_heads(key_value[1], 1))
    return result.reshape(local_rows, -1).astype(jnp.bfloat16)


def plain_body(
    camera_tokens,
    norm_gain,
    query_weight,
    key_weight,
    value_weight,
    query_gain,
    key_gain,
    out_weight,
    up_weight,
    up_bias,
    down_weight,
    down_bias,
    join_gain,
    join_query,
    join_key,
    join_value,
    join_query_gain,
    join_key_gain,
    join_out,
):
    own_rows = camera_tokens.shape[0]
    all_rows = own_rows * lax.axis_size("rows")
    col_rows = all_rows // lax.axis_size("cols")
    attn_width = query_weight.shape[1]
    start_f32 = camera_tokens.astype(jnp.float32)
    normed_all = lax.all_gather(
        normalize(start_f32, norm_gain, shard_moments(start_f32)), "rows", axis=0, tiled=True
    )
    joint_weight = jnp.concatenate((query_weight, key_weight, value_weight, up_weight), 1)
    joint = lax.psum_scatter(
        jnp.dot(normed_all, joint_weight, preferred_element_type=jnp.float32),
        "cols",
        scatter_dimension=0,
        tiled=True,
    )
    up_sum = joint[:, 3 * attn_width :]
    hidden = jax.nn.gelu(up_sum + up_bias, approximate=False).astype(jnp.bfloat16)
    attended = camera_attention(
        head_norm(joint[:, :attn_width], query_gain),
        head_norm(joint[:, attn_width : 2 * attn_width], key_gain),
        joint[:, 2 * attn_width : 3 * attn_width].astype(jnp.bfloat16),
    )
    attn_all, hidden_all = (
        lax.all_gather(attended, "cols", axis=0, tiled=True),
        lax.all_gather(hidden, "cols", axis=0, tiled=True),
    )
    mixed = lax.psum_scatter(
        jnp.dot(attn_all, out_weight, preferred_element_type=jnp.float32)
        + jnp.dot(hidden_all, down_weight, preferred_element_type=jnp.float32),
        "rows",
        scatter_dimension=0,
        tiled=True,
    )
    layer_own = (start_f32 + mixed + down_bias).astype(jnp.bfloat16)
    layer_f32 = layer_own.astype(jnp.float32)
    join_in = lax.all_gather(
        normalize(layer_f32, join_gain, shard_moments(layer_f32)), "rows", axis=0, tiled=True
    )
    join_weight = jnp.concatenate((join_query, join_key, join_value), 1)
    join_joint = lax.psum_scatter(
        jnp.dot(join_in, join_weight, preferred_element_type=jnp.float32),
        "cols",
        scatter_dimension=0,
        tiled=True,
    )
    join_q = head_norm(join_joint[:, :attn_width], join_query_gain)
    join_k = head_norm(join_joint[:, attn_width : 2 * attn_width], join_key_gain)
    join_v = join_joint[:, 2 * attn_width :].astype(jnp.bfloat16)
    heads_here = attn_width // HEAD_DIM
    query_heads = join_q.reshape(col_rows, heads_here, HEAD_DIM)
    inv_root = 1.0 / math.sqrt(HEAD_DIM)
    run_max = jnp.full((heads_here, col_rows), -jnp.inf, jnp.float32)
    run_sum = jnp.zeros((heads_here, col_rows), jnp.float32)
    accum = jnp.zeros((col_rows, heads_here, HEAD_DIM), jnp.float32)
    key_part = lax.all_gather(join_k, "cols", axis=0, tiled=True)
    val_part = lax.all_gather(join_v, "cols", axis=0, tiled=True)
    row_count = key_part.shape[0]
    key_heads = key_part.reshape(row_count, heads_here, HEAD_DIM)
    val_heads = val_part.reshape(row_count, heads_here, HEAD_DIM)
    scores = (
        jnp.einsum("qhd,khd->hqk", query_heads, key_heads, preferred_element_type=jnp.float32)
        * inv_root
    )
    new_max = jnp.max(scores, -1)
    factor = jnp.exp(run_max - new_max)
    weights = jnp.exp(scores - new_max[..., None])
    run_sum = run_sum * factor + jnp.sum(weights, -1)
    accum = accum * jnp.transpose(factor)[..., None] + jnp.einsum(
        "hqk,khd->qhd", weights.astype(jnp.bfloat16), val_heads, preferred_element_type=jnp.float32
    )
    run_max, run_sum, accum = (new_max, run_sum, accum)
    joined_attn = (
        (accum / jnp.transpose(run_sum)[..., None])
        .reshape(col_rows, attn_width)
        .astype(jnp.bfloat16)
    )
    joined_all = lax.all_gather(joined_attn, "cols", axis=0, tiled=True)
    result = lax.psum_scatter(
        jnp.dot(joined_all, join_out, preferred_element_type=jnp.float32),
        "rows",
        scatter_dimension=0,
        tiled=True,
    )
    return (layer_own.astype(jnp.float32) + result).astype(jnp.bfloat16)


F32 = jnp.float32
BF16 = jnp.bfloat16
MESH = pl.DeviceIdType.MESH
VMEM_LIMIT = 66 * 1024 * 1024 - 3 * 1024 * 1024


def each(count, step):
    lax.fori_loop(0, count, lambda i, carry: (step(i), carry)[1], None)


def remote(src, dst, send, recv, device):
    return pltpu.make_async_remote_copy(
        src_ref=src,
        dst_ref=dst,
        send_sem=send,
        recv_sem=recv,
        device_id=device,
        device_id_type=MESH,
    )


def places():
    col = lax.axis_index("cols")
    core = lax.rem(col, 2)
    return col, col + 1 - 2 * core, lax.rem(col + 2, 4)


def greet(cols_away):
    col, row, row_count = lax.axis_index("cols"), lax.axis_index("rows"), lax.axis_size("rows")
    barrier = pltpu.get_barrier_semaphore()
    _, mate, across = places()
    others = {1: mate, 2: across}
    if cols_away == 3:
        others[3] = mate + across - col
    for other in others.values():
        pl.semaphore_signal(barrier, inc=1, device_id={"cols": other}, device_id_type=MESH)

    @pl.when(row > 0)
    def _():
        pl.semaphore_signal(barrier, inc=1, device_id={"rows": row - 1}, device_id_type=MESH)

    @pl.when(row < row_count - 1)
    def _():
        pl.semaphore_signal(barrier, inc=1, device_id={"rows": row + 1}, device_id_type=MESH)

    inner = (row > 0) & (row < row_count - 1)

    @pl.when(inner)
    def _():
        pl.semaphore_wait(barrier, len(others) + 2)

    @pl.when(jnp.logical_not(inner))
    def _():
        pl.semaphore_wait(barrier, len(others) + 1)


def gather_rows(normed, send_r, send_l, arrive):
    row, row_count = lax.axis_index("rows"), lax.axis_size("rows")

    def to_right(block):
        return remote(
            normed.at[block], normed.at[block], send_r.at[block], arrive.at[block], {"rows": row + 1}
        )

    def to_left(block):
        return remote(
            normed.at[block], normed.at[block], send_l.at[block], arrive.at[block], {"rows": row - 1}
        )

    def pass_on(from_left, block):
        if from_left:

            @pl.when(row < row_count - 1)
            def _():
                to_right(block).start()
        else:

            @pl.when(row > 0)
            def _():
                to_left(block).start()

    pass_on(True, row)
    pass_on(False, row)

    def take(away):
        @pl.when(row >= away)
        def _():
            to_right(row - away).wait_recv()
            pass_on(True, row - away)

        @pl.when(row + away < row_count)
        def _():
            to_left(row + away).wait_recv()
            pass_on(False, row + away)

    def finish():
        for block in range(row_count):

            @pl.when((row >= block) & (row < row_count - 1))
            def _():
                to_right(block).wait_send()

            @pl.when((row <= block) & (row > 0))
            def _():
                to_left(block).wait_send()

    return take, finish


def norm_heads(values, scales):
    parts = []
    for start in range(0, values.shape[1], HEAD_DIM):
        part = values[:, start : start + HEAD_DIM]
        mean = jnp.mean(part, -1, keepdims=True)
        var = jnp.mean(part * part, -1, keepdims=True) - mean * mean
        parts.append((part - mean) * lax.rsqrt(var + EPS))
    return (jnp.concatenate(parts, 1) * scales).astype(BF16)


def soft_blend(query, keys, values):
    scores = lax.dot_general(
        query, keys, (((1,), (1,)), ((), ())), preferred_element_type=F32
    ) * (1.0 / math.sqrt(HEAD_DIM))
    weights = jnp.exp(scores - jnp.max(scores, -1, keepdims=True))
    total = jnp.sum(weights, -1, keepdims=True)
    blended = jnp.dot(weights.astype(BF16), values, preferred_element_type=F32)
    return (blended / total).astype(BF16)


def in_kernel(span, has_up, width, *refs):
    refs = list(refs)
    tokens, gain, q_gain, k_gain, wq, wk, wv = refs[:7]
    refs = refs[7:]
    if has_up:
        bias, w_up = refs[:2]
        refs = refs[2:]
    out_a = refs.pop(0)
    if has_up:
        out_u = refs.pop(0)
    normed, moments, m_send, m_recv, z_right, z_left, z_arrive, queries, keys, values = refs[:10]
    groups = [refs[10:25]]
    if has_up:
        groups.append(refs[25:40])
    col, mate, across = places()
    diagonal = mate + across - col
    row, row_count = lax.axis_index("rows"), lax.axis_size("rows")
    own_rows = tokens.shape[0]
    near = row_count // 2

    def load(group, unit, owner, source, start):
        held = group[0]
        columns = pl.ds(pl.multiple_of(start, HEAD_DIM), held.shape[-1])
        return pltpu.make_async_copy(
            source.at[:, columns], held.at[unit * 4 + owner], group[6].at[unit * 4 + owner]
        )

    def loads(group_id, unit, owner, which=None):
        group = groups[group_id]
        wide = group[0].shape[-1]
        if group_id == 0:
            return load(group, unit, owner, (wq, wk, wv)[which], owner * wide)
        return load(group, unit, owner, w_up, owner * (groups[1][5].shape[0] * wide) + unit * wide)

    def start_loads(owner):
        for which in range(3):
            loads(0, which, owner, which).start()
        if has_up:
            each(groups[1][5].shape[0], lambda unit: loads(1, unit, owner).start())

    order = (diagonal, across, mate, col)
    for owner in order:
        start_loads(owner)
    greet(3)

    own = tokens[...].astype(F32)
    lane = lax.broadcasted_iota(jnp.int32, (own_rows, HEAD_DIM), 1)
    mine = jnp.where(
        lane < HEAD_DIM // 2,
        jnp.sum(own, 1, keepdims=True),
        jnp.sum(own * own, 1, keepdims=True),
    )
    moments[3] = mine
    swaps = []
    for slot, other in enumerate((mate, across, diagonal)):
        swap = remote(
            moments.at[3], moments.at[slot], m_send.at[slot], m_recv.at[slot], {"cols": other}
        )
        swap.start()
        swaps.append(swap)
    for swap in swaps:
        swap.wait_recv()
    total = (moments[3] + moments[0]) + (moments[1] + moments[2])
    mean = total[:, :1] / width
    var = total[:, HEAD_DIM // 2 : HEAD_DIM // 2 + 1] / width - mean * mean
    normed[row] = ((own - mean) * lax.rsqrt(var + EPS) * gain[...].reshape(1, -1)).astype(BF16)
    take_rows, finish_rows = gather_rows(normed, z_right, z_left, z_arrive)
    for swap in swaps:
        swap.wait_send()

    def ops(group):
        held, f_send, f_recv, p_send, p_recv, own_sum, _, y_send, y_recv, fs, fr, ps, pr, ys, yr = group

        def product(unit, left, owner, fresh):
            weight = held.at[unit * 4 + owner]
            if fresh:
                pltpu.make_async_copy(weight, weight, group[6].at[unit * 4 + owner]).wait()
            return jnp.dot(left, weight[...], preferred_element_type=F32)

        def first_to_mate(unit, block):
            return remote(
                f_send.at[unit, block],
                f_recv.at[unit, block],
                fs.at[unit, block],
                fr.at[unit, block],
                {"cols": mate},
            )

        def second_to_mate(unit, half):
            return remote(
                p_send.at[unit, half],
                p_recv.at[unit, half],
                ps.at[unit, half],
                pr.at[unit, half],
                {"cols": mate},
            )

        def to_across(unit, block):
            return remote(
                y_send.at[unit, block],
                y_recv.at[unit, block],
                ys.at[unit, block],
                yr.at[unit, block],
                {"cols": across},
            )

        def first(block, fresh):
            def give(unit):
                f_send[unit, block] = product(unit, normed[block], diagonal, fresh).astype(BF16)
                first_to_mate(unit, block).start()

            def send(unit):
                partial = product(unit, normed[block], across, fresh)
                first_to_mate(unit, block).wait_recv()
                y_send[unit, block] = (partial + f_recv[unit, block].astype(F32)).astype(BF16)
                to_across(unit, block).start()

            each(own_sum.shape[0], give)
            each(own_sum.shape[0], send)

        def second(half, fresh):
            def rows_in():
                return normed[pl.ds(half * near, near)].reshape(near * own_rows, normed.shape[-1])

            def give(unit):
                p_send[unit, half] = product(unit, rows_in(), mate, fresh).astype(BF16)
                second_to_mate(unit, half).start()

            def keep(unit):
                partial = product(unit, rows_in(), col, fresh)
                second_to_mate(unit, half).wait_recv()
                own_sum[unit, half] = partial + p_recv[unit, half].astype(F32)

            each(own_sum.shape[0], give)
            each(own_sum.shape[0], keep)

        def final(unit, half):
            for place in range(near):
                to_across(unit, half * near + place).wait_recv()
            arrived = y_recv[unit, pl.ds(half * near, near)].astype(F32)
            return own_sum[unit, half] + arrived.reshape(near * own_rows, -1)

        def finish(unit):
            for block in range(row_count):
                first_to_mate(unit, block).wait_send()
                to_across(unit, block).wait_send()
            for half in range(2):
                second_to_mate(unit, half).wait_send()

        return first, second, final, finish, own_sum.shape[0]

    all_ops = [ops(group) for group in groups]
    home = row // near
    wide = groups[0][0].shape[-1]
    mine = pl.ds(pl.multiple_of(col * wide, HEAD_DIM), wide)
    half_rows = near * own_rows

    def firsts(block, fresh):
        for first, *_ in all_ops:
            first(block, fresh)

    def seconds(half, fresh):
        for _, second, *_ in all_ops:
            second(half, fresh)

    def camera(which):
        rows = pl.ds(pl.multiple_of(which * span, span), span)
        local = pl.ds(pl.multiple_of(lax.rem(which * span, half_rows), span), span)
        for start in range(0, wide, HEAD_DIM):
            head = slice(start, start + HEAD_DIM)
            out_a[which * span // half_rows, local, head] = soft_blend(
                queries[rows, head], keys[rows, head], values[rows, head]
            )

    def joint(half):
        for start in range(0, wide, HEAD_DIM):
            head = slice(start, start + HEAD_DIM)
            rows = pl.ds(pl.multiple_of(half * half_rows, half_rows), half_rows)
            out_a[half, :, head] = soft_blend(queries[rows, head], keys[:, head], values[:, head])

    def finals(half):
        final = all_ops[0][2]
        rows = pl.ds(pl.multiple_of(half * half_rows, half_rows), half_rows)
        queries[rows] = norm_heads(final(0, half), q_gain[mine].reshape(1, -1))
        keys[rows] = norm_heads(final(1, half), k_gain[mine].reshape(1, -1))
        values[rows] = final(2, half).astype(BF16)
        if span < half_rows:
            count = half_rows // span
            each(count, lambda which: camera(half * count + which))
        if has_up:
            up_final = all_ops[1][2]

            def activate(unit):
                raw = up_final(unit, half) + bias[col * out_u.shape[0] + unit]
                out_u[unit, half] = (raw * (1.0 + lax.erf(raw * math.sqrt(0.5))) * 0.5).astype(BF16)

            each(out_u.shape[0], activate)

    firsts(row, True)
    take_rows(1)
    firsts(row + 1 - 2 * lax.rem(row, 2), False)
    seconds(home, True)
    take_rows(2)
    firsts(near - home, False)
    take_rows(3)
    firsts((row_count - 1) * (1 - home), False)
    if has_up:
        finals(home)
        seconds(1 - home, False)
    else:
        seconds(1 - home, False)
        finals(home)
    finals(1 - home)
    if span == 2 * half_rows:
        each(2, joint)
    for first, second, final, finish, count in all_ops:
        each(count, finish)
    finish_rows()


def in_call(name, number, span, tokens, gain, q_gain, k_gain, weights, up=None):
    own_rows, depth = tokens.shape
    all_rows = own_rows * lax.axis_size("rows")
    cols = lax.axis_size("cols")
    wide = weights[0].shape[1] // cols
    groups = [(3, wide)]
    operands = [tokens, gain, q_gain, k_gain, *weights]
    any_spec, vmem_spec = pl.BlockSpec(memory_space=pl.ANY), pl.BlockSpec(memory_space=pltpu.VMEM)
    in_specs = [vmem_spec] * 4 + [any_spec] * 3
    half_rows = all_rows // 2
    out_shape = [jax.ShapeDtypeStruct((2, half_rows, wide), BF16)]
    if up is not None:
        up_bias, up_weight = up
        up_wide = up_tile(up_weight.shape[1] // cols)
        count = up_weight.shape[1] // cols // up_wide
        groups.append((count, up_wide))
        operands += [up_bias.reshape(cols * count, 1, up_wide), up_weight]
        in_specs += [vmem_spec, any_spec]
        out_shape.append(jax.ShapeDtypeStruct((count, 2, half_rows, up_wide), BF16))
    dma = pltpu.SemaphoreType.DMA
    row_count = lax.axis_size("rows")
    scratch = [
        pltpu.VMEM((row_count, own_rows, depth), BF16),
        pltpu.VMEM((4, own_rows, HEAD_DIM), F32),
        dma((3,)),
        dma((3,)),
        dma((row_count,)),
        dma((row_count,)),
        dma((row_count,)),
    ] + [pltpu.VMEM((all_rows, wide), BF16)] * 3
    for count, piece in groups:
        scratch += [
            pltpu.VMEM((count * 4, depth, piece), BF16),
            pltpu.VMEM((count, row_count, own_rows, piece), BF16),
            pltpu.VMEM((count, row_count, own_rows, piece), BF16),
            pltpu.VMEM((count, 2, half_rows, piece), BF16),
            pltpu.VMEM((count, 2, half_rows, piece), BF16),
            pltpu.VMEM((count, 2, half_rows, piece), F32),
            dma((count * 4,)),
            pltpu.VMEM((count, row_count, own_rows, piece), BF16),
            pltpu.VMEM((count, row_count, own_rows, piece), BF16),
            dma((count, row_count)),
            dma((count, row_count)),
            dma((count, 2)),
            dma((count, 2)),
            dma((count, row_count)),
            dma((count, row_count)),
        ]
    return pl.pallas_call(
        functools.partial(in_kernel, span, up is not None, float(depth * cols)),
        name=name,
        out_shape=out_shape,
        in_specs=in_specs,
        out_specs=[vmem_spec] * len(out_shape),
        scratch_shapes=scratch,
        compiler_params=pltpu.CompilerParams(
            collective_id=number, has_side_effects=True, vmem_limit_bytes=VMEM_LIMIT
        ),
    )(*operands)


def out_kernel(has_up, *refs):
    refs = list(refs)
    base, heads, w_out = refs[:3]
    refs = refs[3:]
    if has_up:
        bias, hidden, w_down = refs[:3]
        refs = refs[3:]
    result, accum, right_send, left_send, from_left, from_right = refs[:6]
    r_send, r_recv, l_send, l_recv = refs[6:10]
    groups = [refs[10:18]]
    if has_up:
        groups.append(refs[18:26])
    col, mate, across = places()
    diagonal = mate + across - col
    row, row_count = lax.axis_index("rows"), lax.axis_size("rows")
    own_rows = base.shape[0]
    near = row_count // 2
    owners = (col, mate, across, diagonal)
    sources = [(heads, w_out)]
    if has_up:
        sources.append((hidden, w_down))

    def load(group_id, unit, place):
        held, sem = groups[group_id][0], groups[group_id][1]
        source = sources[group_id][1]
        deep = held.shape[1]
        count = held.shape[0] // 4
        start = pl.multiple_of((owners[place] * count + unit) * deep, HEAD_DIM)
        return pltpu.make_async_copy(
            source.at[pl.ds(start, deep)], held.at[place * count + unit], sem.at[place * count + unit]
        )

    for place in range(4):
        for group_id, group in enumerate(groups):
            each(group[0].shape[0] // 4, lambda unit: load(group_id, unit, place).start())
    greet(2)

    def part_of(ref, stage):
        return ref.at[pl.ds(stage[0], stage[1])]

    def read(ref, stage):
        return part_of(ref, stage)[...].reshape(stage[1] * own_rows, -1)

    def copies(group_id):
        _, _, got, y_send, p_send, f_send, y_recv, p_recv = groups[group_id]
        source = sources[group_id][0]

        def to_across(unit, half):
            return remote(
                part_of(source.at[unit], half),
                part_of(got.at[1, unit], half),
                y_send.at[unit, half[2]],
                y_recv.at[unit, half[2]],
                {"cols": across},
            )

        def to_mate(unit, half):
            return remote(
                part_of(source.at[unit], half),
                part_of(got.at[0, unit], half),
                p_send.at[unit, half[2]],
                p_recv.at[0, unit, half[2]],
                {"cols": mate},
            )

        def forward(unit, half):
            return remote(
                part_of(got.at[1, unit], half),
                part_of(got.at[2, unit], half),
                f_send.at[unit, half[2]],
                p_recv.at[1, unit, half[2]],
                {"cols": mate},
            )

        return to_across, to_mate, forward, groups[group_id][0].shape[0] // 4

    moves = [copies(group_id) for group_id in range(len(groups))]
    home = row // near
    pair = row + 1 - 2 * lax.rem(row, 2)
    stages = (((1 - home) * near, near, 0), (pair, 1, 1), (row, 1, 2))
    for half in stages:
        for to_across, to_mate, forward, count in moves:
            each(count, lambda unit: to_across(unit, half).start())
            each(count, lambda unit: to_mate(unit, half).start())

    def add(group_id, unit, place, half, fresh, piece, begin=False):
        if fresh:
            load(group_id, unit, place).wait()
        held = groups[group_id][0]
        count = held.shape[0] // 4
        part = jnp.dot(piece, held[place * count + unit], preferred_element_type=F32)
        part = part.reshape(half[1], own_rows, -1)
        if begin:
            part_of(accum, half)[...] = part
        else:
            part_of(accum, half)[...] += part

    def near_chunks(half, fresh):
        for group_id, (to_across, to_mate, forward, count) in enumerate(moves):
            source, got = sources[group_id][0], groups[group_id][2]
            if group_id == 0:
                add(0, 0, 0, half, fresh, read(source.at[0], half), True)
            else:
                each(count, lambda unit: add(group_id, unit, 0, half, fresh, read(source.at[unit], half)))

            def from_mate(unit):
                to_mate(unit, half).wait_recv()
                add(group_id, unit, 1, half, fresh, read(got.at[0, unit], half))

            each(count, from_mate)

    def far_chunks(half, fresh):
        for group_id, (to_across, to_mate, forward, count) in enumerate(moves):
            got = groups[group_id][2]

            def from_across(unit):
                to_across(unit, half).wait_recv()
                forward(unit, half).start()
                add(group_id, unit, 2, half, fresh, read(got.at[1, unit], half))
                forward(unit, half).wait_recv()
                add(group_id, unit, 3, half, fresh, read(got.at[2, unit], half))

            each(count, from_across)

    piece_wide = from_left.shape[-1]
    pieces = from_left.shape[1]

    def term(block, piece):
        return accum[block, :, piece * piece_wide : (piece + 1) * piece_wide]

    def to_right(block, piece):
        return remote(
            right_send.at[block, piece],
            from_left.at[block, piece],
            r_send.at[block, piece],
            r_recv.at[block, piece],
            {"rows": row + 1},
        )

    def to_left(block, piece):
        return remote(
            left_send.at[block, piece],
            from_right.at[block, piece],
            l_send.at[block, piece],
            l_recv.at[block, piece],
            {"rows": row - 1},
        )

    def run(move, send, arrived, block, edge):
        for piece in range(pieces):

            @pl.when(row == edge)
            def _():
                send[block, piece] = term(block, piece).astype(BF16)

            @pl.when(row != edge)
            def _():
                move(block, piece).wait_recv()
                send[block, piece] = (
                    term(block, piece) + arrived[block, piece].astype(F32)
                ).astype(BF16)

            move(block, piece).start()

    def run_right(block):
        run(to_right, right_send, from_left, block, 0)

    def run_left(block):
        run(to_left, left_send, from_right, block, row_count - 1)

    def send_far(from_end):
        at_end = (row == 0) | (row == row_count - 1)
        now = at_end if from_end else jnp.logical_not(at_end)

        @pl.when(now & (row < near))
        def _():
            each(near, lambda step: run_right(row_count - 1 - step))

        @pl.when(now & (row >= near))
        def _():
            each(near, run_left)

    near_chunks(stages[0], True)
    far_chunks(stages[0], True)
    send_far(True)
    near_chunks(stages[1], False)
    if has_up:
        far_chunks(stages[1], False)
        send_far(False)
        near_chunks(stages[2], False)
    else:
        far_chunks(stages[1], False)
        near_chunks(stages[2], False)
        send_far(False)

    @pl.when(row < pair)
    def _():
        run_right(pair)

    @pl.when(row > pair)
    def _():
        run_left(pair)

    far_chunks(stages[2], False)
    for piece in range(pieces):
        columns = slice(piece * piece_wide, (piece + 1) * piece_wide)
        total = term(row, piece) + base[:, columns].astype(F32)
        if has_up:
            total += bias[columns].reshape(1, -1)
        accum[row, :, columns] = total

        @pl.when(row > 0)
        def _():
            to_right(row, piece).wait_recv()
            accum[row, :, columns] += from_left[row, piece].astype(F32)

        @pl.when(row < row_count - 1)
        def _():
            to_left(row, piece).wait_recv()
            accum[row, :, columns] += from_right[row, piece].astype(F32)

        result[:, columns] = term(row, piece).astype(BF16)

    def sent(block):
        for piece in range(pieces):

            @pl.when(row < block)
            def _():
                to_right(block, piece).wait_send()

            @pl.when(row > block)
            def _():
                to_left(block, piece).wait_send()

    each(row_count, sent)

    for to_across, to_mate, forward, count in moves:

        def finish(unit):
            for half in stages:
                to_across(unit, half).wait_send()
                to_mate(unit, half).wait_send()
                forward(unit, half).wait_send()

        each(count, finish)


def out_call(name, number, base, heads, w_out, up=None):
    own_rows, width = base.shape
    _, half_rows, wide = heads.shape
    row_count = lax.axis_size("rows")
    any_spec, vmem_spec = pl.BlockSpec(memory_space=pl.ANY), pl.BlockSpec(memory_space=pltpu.VMEM)
    row_count = lax.axis_size("rows")
    operands = [base, heads.reshape(1, row_count, own_rows, wide), w_out]
    in_specs = [vmem_spec, vmem_spec, any_spec]
    groups = [(1, wide)]
    if up is not None:
        bias, hidden, w_down = up
        operands += [bias, hidden.reshape(hidden.shape[0], row_count, own_rows, -1), w_down]
        in_specs += [vmem_spec, vmem_spec, any_spec]
        groups.append((hidden.shape[0], hidden.shape[3]))
    dma = pltpu.SemaphoreType.DMA
    piece_wide = up_tile(width)
    pieces = width // piece_wide
    block = pltpu.VMEM((row_count, pieces, own_rows, piece_wide), BF16)
    scratch = [pltpu.VMEM((row_count, own_rows, width), F32)] + [block] * 4 + [dma((row_count, pieces))] * 4
    for count, piece in groups:
        scratch += [
            pltpu.VMEM((4 * count, piece, width), BF16),
            dma((4 * count,)),
            pltpu.VMEM((3, count, row_count, own_rows, piece), BF16),
            dma((count, 3)),
            dma((count, 3)),
            dma((count, 3)),
            dma((count, 3)),
            dma((2, count, 3)),
        ]
    return pl.pallas_call(
        functools.partial(out_kernel, up is not None),
        name=name,
        out_shape=jax.ShapeDtypeStruct((own_rows, width), BF16),
        in_specs=in_specs,
        out_specs=vmem_spec,
        scratch_shapes=scratch,
        compiler_params=pltpu.CompilerParams(
            collective_id=number, has_side_effects=True, vmem_limit_bytes=VMEM_LIMIT
        ),
    )(*operands)


def up_tile(columns):
    for tile in (4 * HEAD_DIM, 2 * HEAD_DIM, HEAD_DIM):
        if columns % tile == 0:
            return tile
    return columns


def kernel_body(
    camera_tokens,
    norm_gain,
    query_weight,
    key_weight,
    value_weight,
    query_gain,
    key_gain,
    out_weight,
    up_weight,
    up_bias,
    down_weight,
    down_bias,
    join_gain,
    join_query,
    join_key,
    join_value,
    join_query_gain,
    join_key_gain,
    join_out,
):
    all_rows = camera_tokens.shape[0] * lax.axis_size("rows")
    heads, hidden = in_call(
        "camera_in",
        0,
        TOK_CAM,
        camera_tokens,
        norm_gain,
        query_gain,
        key_gain,
        (query_weight, key_weight, value_weight),
        (up_bias, up_weight),
    )
    layer_own = out_call(
        "camera_out", 1, camera_tokens, heads, out_weight, (down_bias, hidden, down_weight)
    )
    (joined,) = in_call(
        "join_in",
        2,
        all_rows,
        layer_own,
        join_gain,
        join_query_gain,
        join_key_gain,
        (join_query, join_key, join_value),
    )
    return out_call("join_out", 3, layer_own, joined, join_out)


def fits(mesh):
    cols, rows = mesh.shape["cols"], mesh.shape["rows"]
    return cols == 4 and rows == 4 and D % (rows * cols * HEAD_DIM) == 0


def solution(mesh):
    in_specs = (
        P(("groups", "rows"), "cols"),
        P("cols"),
        P("cols", "rows"),
        P("cols", "rows"),
        P("cols", "rows"),
        P("rows"),
        P("rows"),
        P("rows", "cols"),
        P("cols", "rows"),
        P("rows"),
        P("rows", "cols"),
        P("cols"),
        P("cols"),
        P("cols", "rows"),
        P("cols", "rows"),
        P("cols", "rows"),
        P("rows"),
        P("rows"),
        P("rows", "cols"),
    )
    out_specs = P(("groups", "rows"), "cols")
    body = kernel_body if fits(mesh) else plain_body
    return jax.shard_map(body, mesh=mesh, in_specs=in_specs, out_specs=out_specs, check_vma=False)
```

```python
import functools
import math

import jax
import jax.numpy as jnp
from jax import lax
from jax.experimental import pallas as pl
from jax.experimental.pallas import tpu as pltpu
from jax.sharding import PartitionSpec as P

HEAD_DIM = 128
TOK_CAM = 64
D = 6144


EPS = 1e-06


def partner_2(array, axis, bit):
    return lax.ppermute(array, axis, [(i, i ^ 1 << bit) for i in range(lax.axis_size(axis))])


def normalize(values, scales, moments):
    row_mean = moments[0] / D
    row_var = moments[1] / D - row_mean * row_mean
    return ((values - row_mean[:, None]) * lax.rsqrt(row_var[:, None] + EPS) * scales).astype(
        jnp.bfloat16
    )


def shard_moments(values):
    return lax.psum((jnp.sum(values, 1), jnp.sum(values * values, 1)), "cols")


def head_norm(values, scales):
    row_count = values.shape[0]
    grouped = values.reshape(row_count, -1, HEAD_DIM)
    row_mean = jnp.mean(grouped, -1, keepdims=True)
    row_var = jnp.mean(grouped * grouped, -1, keepdims=True) - row_mean * row_mean
    normed = (grouped - row_mean) * lax.rsqrt(row_var + EPS)
    return (normed.reshape(row_count, -1) * scales).astype(jnp.bfloat16)


def attend(queries, key_rows, val_rows):
    inv_root = 1.0 / math.sqrt(HEAD_DIM)
    scores = (
        jnp.einsum("bqhd,bkhd->bhqk", queries, key_rows, preferred_element_type=jnp.float32)
        * inv_root
    )
    row_max = jnp.max(scores, -1, keepdims=True)
    weights = jnp.exp(scores - row_max)
    row_sum = jnp.sum(weights, -1)
    blended = jnp.einsum(
        "bhqk,bkhd->bqhd",
        weights.astype(jnp.bfloat16),
        val_rows,
        preferred_element_type=jnp.float32,
    )
    return blended / jnp.transpose(row_sum, (0, 2, 1))[..., None]


def to_heads(matrix, blocks):
    return matrix.reshape(blocks, -1, matrix.shape[1] // HEAD_DIM, HEAD_DIM)


def camera_attention(queries, key_rows, val_rows):
    local_rows = queries.shape[0]
    if local_rows >= TOK_CAM:
        blocks = local_rows // TOK_CAM
        result = attend(
            to_heads(queries, blocks), to_heads(key_rows, blocks), to_heads(val_rows, blocks)
        )
    else:
        cam_span = TOK_CAM // local_rows
        position = lax.axis_index("cols")
        key_value = jnp.stack((key_rows, val_rows))
        for which_bit in range(cam_span.bit_length() - 1):
            partner = partner_2(key_value, "cols", which_bit)
            is_lower = position >> which_bit & 1 == 0
            key_value = jnp.where(
                is_lower,
                jnp.concatenate((key_value, partner), 1),
                jnp.concatenate((partner, key_value), 1),
            )
        result = attend(to_heads(queries, 1), to_heads(key_value[0], 1), to_heads(key_value[1], 1))
    return result.reshape(local_rows, -1).astype(jnp.bfloat16)


def plain_body(
    camera_tokens,
    norm_gain,
    query_weight,
    key_weight,
    value_weight,
    query_gain,
    key_gain,
    out_weight,
    up_weight,
    up_bias,
    down_weight,
    down_bias,
    join_gain,
    join_query,
    join_key,
    join_value,
    join_query_gain,
    join_key_gain,
    join_out,
):
    own_rows = camera_tokens.shape[0]
    all_rows = own_rows * lax.axis_size("rows")
    col_rows = all_rows // lax.axis_size("cols")
    attn_width = query_weight.shape[1]
    start_f32 = camera_tokens.astype(jnp.float32)
    normed_all = lax.all_gather(
        normalize(start_f32, norm_gain, shard_moments(start_f32)), "rows", axis=0, tiled=True
    )
    joint_weight = jnp.concatenate((query_weight, key_weight, value_weight, up_weight), 1)
    joint = lax.psum_scatter(
        jnp.dot(normed_all, joint_weight, preferred_element_type=jnp.float32),
        "cols",
        scatter_dimension=0,
        tiled=True,
    )
    up_sum = joint[:, 3 * attn_width :]
    hidden = jax.nn.gelu(up_sum + up_bias, approximate=False).astype(jnp.bfloat16)
    attended = camera_attention(
        head_norm(joint[:, :attn_width], query_gain),
        head_norm(joint[:, attn_width : 2 * attn_width], key_gain),
        joint[:, 2 * attn_width : 3 * attn_width].astype(jnp.bfloat16),
    )
    attn_all, hidden_all = (
        lax.all_gather(attended, "cols", axis=0, tiled=True),
        lax.all_gather(hidden, "cols", axis=0, tiled=True),
    )
    mixed = lax.psum_scatter(
        jnp.dot(attn_all, out_weight, preferred_element_type=jnp.float32)
        + jnp.dot(hidden_all, down_weight, preferred_element_type=jnp.float32),
        "rows",
        scatter_dimension=0,
        tiled=True,
    )
    layer_own = (start_f32 + mixed + down_bias).astype(jnp.bfloat16)
    layer_f32 = layer_own.astype(jnp.float32)
    join_in = lax.all_gather(
        normalize(layer_f32, join_gain, shard_moments(layer_f32)), "rows", axis=0, tiled=True
    )
    join_weight = jnp.concatenate((join_query, join_key, join_value), 1)
    join_joint = lax.psum_scatter(
        jnp.dot(join_in, join_weight, preferred_element_type=jnp.float32),
        "cols",
        scatter_dimension=0,
        tiled=True,
    )
    join_q = head_norm(join_joint[:, :attn_width], join_query_gain)
    join_k = head_norm(join_joint[:, attn_width : 2 * attn_width], join_key_gain)
    join_v = join_joint[:, 2 * attn_width :].astype(jnp.bfloat16)
    heads_here = attn_width // HEAD_DIM
    query_heads = join_q.reshape(col_rows, heads_here, HEAD_DIM)
    inv_root = 1.0 / math.sqrt(HEAD_DIM)
    run_max = jnp.full((heads_here, col_rows), -jnp.inf, jnp.float32)
    run_sum = jnp.zeros((heads_here, col_rows), jnp.float32)
    accum = jnp.zeros((col_rows, heads_here, HEAD_DIM), jnp.float32)
    key_part = lax.all_gather(join_k, "cols", axis=0, tiled=True)
    val_part = lax.all_gather(join_v, "cols", axis=0, tiled=True)
    row_count = key_part.shape[0]
    key_heads = key_part.reshape(row_count, heads_here, HEAD_DIM)
    val_heads = val_part.reshape(row_count, heads_here, HEAD_DIM)
    scores = (
        jnp.einsum("qhd,khd->hqk", query_heads, key_heads, preferred_element_type=jnp.float32)
        * inv_root
    )
    new_max = jnp.max(scores, -1)
    factor = jnp.exp(run_max - new_max)
    weights = jnp.exp(scores - new_max[..., None])
    run_sum = run_sum * factor + jnp.sum(weights, -1)
    accum = accum * jnp.transpose(factor)[..., None] + jnp.einsum(
        "hqk,khd->qhd", weights.astype(jnp.bfloat16), val_heads, preferred_element_type=jnp.float32
    )
    run_max, run_sum, accum = (new_max, run_sum, accum)
    joined_attn = (
        (accum / jnp.transpose(run_sum)[..., None])
        .reshape(col_rows, attn_width)
        .astype(jnp.bfloat16)
    )
    joined_all = lax.all_gather(joined_attn, "cols", axis=0, tiled=True)
    result = lax.psum_scatter(
        jnp.dot(joined_all, join_out, preferred_element_type=jnp.float32),
        "rows",
        scatter_dimension=0,
        tiled=True,
    )
    return (layer_own.astype(jnp.float32) + result).astype(jnp.bfloat16)


F32 = jnp.float32
BF16 = jnp.bfloat16
MESH = pl.DeviceIdType.MESH
VMEM_LIMIT = 66 * 1024 * 1024 - 3 * 1024 * 1024


def each(count, step):
    lax.fori_loop(0, count, lambda i, carry: (step(i), carry)[1], None)


def remote(src, dst, send, recv, device):
    return pltpu.make_async_remote_copy(
        src_ref=src,
        dst_ref=dst,
        send_sem=send,
        recv_sem=recv,
        device_id=device,
        device_id_type=MESH,
    )


def places():
    col = lax.axis_index("cols")
    core = lax.rem(col, 2)
    return col, col + 1 - 2 * core, lax.rem(col + 2, 4)


def greet(cols_away):
    col, row, row_count = lax.axis_index("cols"), lax.axis_index("rows"), lax.axis_size("rows")
    barrier = pltpu.get_barrier_semaphore()
    _, mate, across = places()
    others = {1: mate, 2: across}
    if cols_away == 3:
        others[3] = mate + across - col
    for other in others.values():
        pl.semaphore_signal(barrier, inc=1, device_id={"cols": other}, device_id_type=MESH)

    @pl.when(row > 0)
    def _():
        pl.semaphore_signal(barrier, inc=1, device_id={"rows": row - 1}, device_id_type=MESH)

    @pl.when(row < row_count - 1)
    def _():
        pl.semaphore_signal(barrier, inc=1, device_id={"rows": row + 1}, device_id_type=MESH)

    inner = (row > 0) & (row < row_count - 1)

    @pl.when(inner)
    def _():
        pl.semaphore_wait(barrier, len(others) + 2)

    @pl.when(jnp.logical_not(inner))
    def _():
        pl.semaphore_wait(barrier, len(others) + 1)


def gather_rows(normed, send_r, send_l, arrive):
    row, row_count = lax.axis_index("rows"), lax.axis_size("rows")

    def to_right(block):
        return remote(
            normed.at[block], normed.at[block], send_r.at[block], arrive.at[block], {"rows": row + 1}
        )

    def to_left(block):
        return remote(
            normed.at[block], normed.at[block], send_l.at[block], arrive.at[block], {"rows": row - 1}
        )

    def pass_on(from_left, block):
        if from_left:

            @pl.when(row < row_count - 1)
            def _():
                to_right(block).start()
        else:

            @pl.when(row > 0)
            def _():
                to_left(block).start()

    pass_on(True, row)
    pass_on(False, row)

    def take(away):
        @pl.when(row >= away)
        def _():
            to_right(row - away).wait_recv()
            pass_on(True, row - away)

        @pl.when(row + away < row_count)
        def _():
            to_left(row + away).wait_recv()
            pass_on(False, row + away)

    def finish():
        for block in range(row_count):

            @pl.when((row >= block) & (row < row_count - 1))
            def _():
                to_right(block).wait_send()

            @pl.when((row <= block) & (row > 0))
            def _():
                to_left(block).wait_send()

    return take, finish


def norm_heads(values, scales):
    parts = []
    for start in range(0, values.shape[1], HEAD_DIM):
        part = values[:, start : start + HEAD_DIM]
        mean = jnp.mean(part, -1, keepdims=True)
        var = jnp.mean(part * part, -1, keepdims=True) - mean * mean
        parts.append((part - mean) * lax.rsqrt(var + EPS))
    return (jnp.concatenate(parts, 1) * scales).astype(BF16)


def soft_blend(query, keys, values):
    scores = lax.dot_general(
        query, keys, (((1,), (1,)), ((), ())), preferred_element_type=F32
    ) * (1.0 / math.sqrt(HEAD_DIM))
    weights = jnp.exp(scores - jnp.max(scores, -1, keepdims=True))
    total = jnp.sum(weights, -1, keepdims=True)
    blended = jnp.dot(weights.astype(BF16), values, preferred_element_type=F32)
    return (blended / total).astype(BF16)


def in_kernel(span, has_up, width, *refs, follow=None):
    refs = list(refs)
    tokens, gain, q_gain, k_gain, wq, wk, wv = refs[:7]
    refs = refs[7:]
    if has_up:
        bias, w_up = refs[:2]
        refs = refs[2:]
    out_a = refs.pop(0)
    if has_up:
        out_u = refs.pop(0)
    normed, moments, m_send, m_recv, z_right, z_left, z_arrive, queries, keys, values = refs[:10]
    groups = [refs[10:25]]
    if has_up:
        groups.append(refs[25:40])
    col, mate, across = places()
    diagonal = mate + across - col
    row, row_count = lax.axis_index("rows"), lax.axis_size("rows")
    own_rows = tokens.shape[0]
    near = row_count // 2

    def load(group, unit, owner, source, start):
        held = group[0]
        columns = pl.ds(pl.multiple_of(start, HEAD_DIM), held.shape[-1])
        return pltpu.make_async_copy(
            source.at[:, columns], held.at[unit * 4 + owner], group[6].at[unit * 4 + owner]
        )

    def loads(group_id, unit, owner, which=None):
        group = groups[group_id]
        wide = group[0].shape[-1]
        if group_id == 0:
            return load(group, unit, owner, (wq, wk, wv)[which], owner * wide)
        return load(group, unit, owner, w_up, owner * (groups[1][5].shape[0] * wide) + unit * wide)

    def start_loads(owner):
        for which in range(3):
            loads(0, which, owner, which).start()
        if has_up:
            each(groups[1][5].shape[0], lambda unit: loads(1, unit, owner).start())

    order = (diagonal, across, mate, col)
    for owner in order:
        start_loads(owner)
    greet(3)

    own = tokens[...].astype(F32)
    lane = lax.broadcasted_iota(jnp.int32, (own_rows, HEAD_DIM), 1)
    mine = jnp.where(
        lane < HEAD_DIM // 2,
        jnp.sum(own, 1, keepdims=True),
        jnp.sum(own * own, 1, keepdims=True),
    )
    moments[3] = mine
    swaps = []
    for slot, other in enumerate((mate, across, diagonal)):
        swap = remote(
            moments.at[3], moments.at[slot], m_send.at[slot], m_recv.at[slot], {"cols": other}
        )
        swap.start()
        swaps.append(swap)
    for swap in swaps:
        swap.wait_recv()
    total = (moments[3] + moments[0]) + (moments[1] + moments[2])
    mean = total[:, :1] / width
    var = total[:, HEAD_DIM // 2 : HEAD_DIM // 2 + 1] / width - mean * mean
    normed[row] = ((own - mean) * lax.rsqrt(var + EPS) * gain[...].reshape(1, -1)).astype(BF16)
    take_rows, finish_rows = gather_rows(normed, z_right, z_left, z_arrive)
    for swap in swaps:
        swap.wait_send()

    def ops(group):
        held, f_send, f_recv, p_send, p_recv, own_sum, _, y_send, y_recv, fs, fr, ps, pr, ys, yr = group

        def product(unit, left, owner, fresh):
            weight = held.at[unit * 4 + owner]
            if fresh:
                pltpu.make_async_copy(weight, weight, group[6].at[unit * 4 + owner]).wait()
            return jnp.dot(left, weight[...], preferred_element_type=F32)

        def first_to_mate(unit, block):
            return remote(
                f_send.at[unit, block],
                f_recv.at[unit, block],
                fs.at[unit, block],
                fr.at[unit, block],
                {"cols": mate},
            )

        def second_to_mate(unit, half):
            return remote(
                p_send.at[unit, half],
                p_recv.at[unit, half],
                ps.at[unit, half],
                pr.at[unit, half],
                {"cols": mate},
            )

        def to_across(unit, block):
            return remote(
                y_send.at[unit, block],
                y_recv.at[unit, block],
                ys.at[unit, block],
                yr.at[unit, block],
                {"cols": across},
            )

        def first(block, fresh):
            def give(unit):
                f_send[unit, block] = product(unit, normed[block], diagonal, fresh).astype(BF16)
                first_to_mate(unit, block).start()

            def send(unit):
                partial = product(unit, normed[block], across, fresh)
                first_to_mate(unit, block).wait_recv()
                y_send[unit, block] = (partial + f_recv[unit, block].astype(F32)).astype(BF16)
                to_across(unit, block).start()

            each(own_sum.shape[0], give)
            each(own_sum.shape[0], send)

        def second(half, fresh):
            def rows_in():
                return normed[pl.ds(half * near, near)].reshape(near * own_rows, normed.shape[-1])

            def give(unit):
                p_send[unit, half] = product(unit, rows_in(), mate, fresh).astype(BF16)
                second_to_mate(unit, half).start()

            def keep(unit):
                partial = product(unit, rows_in(), col, fresh)
                second_to_mate(unit, half).wait_recv()
                own_sum[unit, half] = partial + p_recv[unit, half].astype(F32)

            each(own_sum.shape[0], give)
            each(own_sum.shape[0], keep)

        def final(unit, half):
            for place in range(near):
                to_across(unit, half * near + place).wait_recv()
            arrived = y_recv[unit, pl.ds(half * near, near)].astype(F32)
            return own_sum[unit, half] + arrived.reshape(near * own_rows, -1)

        def finish(unit):
            for block in range(row_count):
                first_to_mate(unit, block).wait_send()
                to_across(unit, block).wait_send()
            for half in range(2):
                second_to_mate(unit, half).wait_send()

        return first, second, final, finish, own_sum.shape[0]

    all_ops = [ops(group) for group in groups]
    home = row // near
    wide = groups[0][0].shape[-1]
    mine = pl.ds(pl.multiple_of(col * wide, HEAD_DIM), wide)
    half_rows = near * own_rows

    def firsts(block, fresh):
        for first, *_ in all_ops:
            first(block, fresh)

    def seconds(half, fresh):
        for _, second, *_ in all_ops:
            second(half, fresh)

    def camera(which):
        rows = pl.ds(pl.multiple_of(which * span, span), span)
        local = pl.ds(pl.multiple_of(lax.rem(which * span, half_rows), span), span)
        for start in range(0, wide, HEAD_DIM):
            head = slice(start, start + HEAD_DIM)
            out_a[which * span // half_rows, local, head] = soft_blend(
                queries[rows, head], keys[rows, head], values[rows, head]
            )

    def joint(half):
        for start in range(0, wide, HEAD_DIM):
            head = slice(start, start + HEAD_DIM)
            rows = pl.ds(pl.multiple_of(half * half_rows, half_rows), half_rows)
            blended = soft_blend(queries[rows, head], keys[:, head], values[:, head])
            out_a[0, pl.ds(half * near, near), :, head] = blended.reshape(near, own_rows, HEAD_DIM)

    def finals(half):
        final = all_ops[0][2]
        rows = pl.ds(pl.multiple_of(half * half_rows, half_rows), half_rows)
        queries[rows] = norm_heads(final(0, half), q_gain[mine].reshape(1, -1))
        keys[rows] = norm_heads(final(1, half), k_gain[mine].reshape(1, -1))
        values[rows] = final(2, half).astype(BF16)
        if span < half_rows:
            count = half_rows // span
            each(count, lambda which: camera(half * count + which))
        if has_up:
            up_final = all_ops[1][2]

            def activate(unit):
                raw = up_final(unit, half) + bias[col * out_u.shape[0] + unit]
                out_u[unit, half] = (raw * (1.0 + lax.erf(raw * math.sqrt(0.5))) * 0.5).astype(BF16)

            each(out_u.shape[0], activate)

    firsts(row, True)
    take_rows(1)
    firsts(row + 1 - 2 * lax.rem(row, 2), False)
    seconds(home, True)
    take_rows(2)
    firsts(near - home, False)
    take_rows(3)
    firsts((row_count - 1) * (1 - home), False)
    if has_up:
        finals(home)
        seconds(1 - home, False)
    else:
        seconds(1 - home, False)
        finals(home)
    finals(1 - home)
    if follow is not None:
        follow(joint)
    for first, second, final, finish, count in all_ops:
        each(count, finish)
    finish_rows()


def in_call(name, number, span, tokens, gain, q_gain, k_gain, weights, up=None, join=None):
    own_rows, depth = tokens.shape
    all_rows = own_rows * lax.axis_size("rows")
    cols = lax.axis_size("cols")
    wide = weights[0].shape[1] // cols
    groups = [(3, wide)]
    operands = [tokens, gain, q_gain, k_gain, *weights]
    any_spec, vmem_spec = pl.BlockSpec(memory_space=pl.ANY), pl.BlockSpec(memory_space=pltpu.VMEM)
    in_specs = [vmem_spec] * 4 + [any_spec] * 3
    half_rows = all_rows // 2
    out_shape = [jax.ShapeDtypeStruct((2, half_rows, wide), BF16)]
    if up is not None:
        up_bias, up_weight = up
        up_wide = up_tile(up_weight.shape[1] // cols)
        count = up_weight.shape[1] // cols // up_wide
        groups.append((count, up_wide))
        operands += [up_bias.reshape(cols * count, 1, up_wide), up_weight]
        in_specs += [vmem_spec, any_spec]
        out_shape.append(jax.ShapeDtypeStruct((count, 2, half_rows, up_wide), BF16))
    dma = pltpu.SemaphoreType.DMA
    row_count = lax.axis_size("rows")
    scratch = [
        pltpu.VMEM((row_count, own_rows, depth), BF16),
        pltpu.VMEM((4, own_rows, HEAD_DIM), F32),
        dma((3,)),
        dma((3,)),
        dma((row_count,)),
        dma((row_count,)),
        dma((row_count,)),
    ] + [pltpu.VMEM((all_rows, wide), BF16)] * 3
    for count, piece in groups:
        scratch += [
            pltpu.VMEM((count * 4, depth, piece), BF16),
            pltpu.VMEM((count, row_count, own_rows, piece), BF16),
            pltpu.VMEM((count, row_count, own_rows, piece), BF16),
            pltpu.VMEM((count, 2, half_rows, piece), BF16),
            pltpu.VMEM((count, 2, half_rows, piece), BF16),
            pltpu.VMEM((count, 2, half_rows, piece), F32),
            dma((count * 4,)),
            pltpu.VMEM((count, row_count, own_rows, piece), BF16),
            pltpu.VMEM((count, row_count, own_rows, piece), BF16),
            dma((count, row_count)),
            dma((count, row_count)),
            dma((count, 2)),
            dma((count, 2)),
            dma((count, row_count)),
            dma((count, row_count)),
        ]
    if join is not None:
        base_scratch = out_scratch([(1, wide)], own_rows, join.shape[1], row_count)
        return pl.pallas_call(
            functools.partial(join_kernel, span, float(depth * cols)),
            name=name,
            out_shape=jax.ShapeDtypeStruct((own_rows, join.shape[1]), BF16),
            in_specs=in_specs + [any_spec],
            out_specs=vmem_spec,
            scratch_shapes=[pltpu.VMEM((1, row_count, own_rows, wide), BF16)] + scratch + base_scratch,
            compiler_params=pltpu.CompilerParams(
                collective_id=number, has_side_effects=True, vmem_limit_bytes=VMEM_LIMIT
            ),
        )(*operands, join)
    return pl.pallas_call(
        functools.partial(in_kernel, span, up is not None, float(depth * cols)),
        name=name,
        out_shape=out_shape,
        in_specs=in_specs,
        out_specs=[vmem_spec] * len(out_shape),
        scratch_shapes=scratch,
        compiler_params=pltpu.CompilerParams(
            collective_id=number, has_side_effects=True, vmem_limit_bytes=VMEM_LIMIT
        ),
    )(*operands)


def out_kernel(has_up, *refs):
    for _ in out_steps(has_up, {}, *refs):
        pass


def join_kernel(span, width, tokens, gain, q_gain, k_gain, wq, wk, wv, w_out, result, heads, *rest):
    later = {}
    steps = out_steps(False, later, tokens, heads, w_out, result, *rest[25:])
    next(steps)

    def follow(joint):
        later["joint"] = joint
        for _ in steps:
            pass

    in_kernel(
        span, False, width, tokens, gain, q_gain, k_gain, wq, wk, wv, heads, *rest[:25], follow=follow
    )


def out_steps(has_up, later, *refs):
    refs = list(refs)
    base, heads, w_out = refs[:3]
    refs = refs[3:]
    if has_up:
        bias, hidden, w_down = refs[:3]
        refs = refs[3:]
    result, accum, right_send, left_send, from_left, from_right = refs[:6]
    r_send, r_recv, l_send, l_recv = refs[6:10]
    groups = [refs[10:18]]
    if has_up:
        groups.append(refs[18:26])
    col, mate, across = places()
    diagonal = mate + across - col
    row, row_count = lax.axis_index("rows"), lax.axis_size("rows")
    own_rows = base.shape[0]
    near = row_count // 2
    owners = (col, mate, across, diagonal)
    sources = [(heads, w_out)]
    if has_up:
        sources.append((hidden, w_down))

    def load(group_id, unit, place):
        held, sem = groups[group_id][0], groups[group_id][1]
        source = sources[group_id][1]
        deep = held.shape[1]
        count = held.shape[0] // 4
        start = pl.multiple_of((owners[place] * count + unit) * deep, HEAD_DIM)
        return pltpu.make_async_copy(
            source.at[pl.ds(start, deep)], held.at[place * count + unit], sem.at[place * count + unit]
        )

    for place in range(4):
        for group_id, group in enumerate(groups):
            each(group[0].shape[0] // 4, lambda unit: load(group_id, unit, place).start())
    yield
    joint = later.get("joint")
    if joint is None:
        greet(2)

    def part_of(ref, stage):
        return ref.at[pl.ds(stage[0], stage[1])]

    def read(ref, stage):
        return part_of(ref, stage)[...].reshape(stage[1] * own_rows, -1)

    def copies(group_id):
        _, _, got, y_send, p_send, f_send, y_recv, p_recv = groups[group_id]
        source = sources[group_id][0]

        def to_across(unit, half):
            return remote(
                part_of(source.at[unit], half),
                part_of(got.at[1, unit], half),
                y_send.at[unit, half[2]],
                y_recv.at[unit, half[2]],
                {"cols": across},
            )

        def to_mate(unit, half):
            return remote(
                part_of(source.at[unit], half),
                part_of(got.at[0, unit], half),
                p_send.at[unit, half[2]],
                p_recv.at[0, unit, half[2]],
                {"cols": mate},
            )

        def forward(unit, half):
            return remote(
                part_of(got.at[1, unit], half),
                part_of(got.at[2, unit], half),
                f_send.at[unit, half[2]],
                p_recv.at[1, unit, half[2]],
                {"cols": mate},
            )

        return to_across, to_mate, forward, groups[group_id][0].shape[0] // 4

    moves = [copies(group_id) for group_id in range(len(groups))]
    home = row // near
    pair = row + 1 - 2 * lax.rem(row, 2)
    stages = (((1 - home) * near, near, 0), (pair, 1, 1), (row, 1, 2))

    def share(half):
        for to_across, to_mate, forward, count in moves:
            each(count, lambda unit: to_across(unit, half).start())
            each(count, lambda unit: to_mate(unit, half).start())

    if joint is not None:
        joint(1 - home)
    share(stages[0])
    if joint is None:
        share(stages[1])
        share(stages[2])

    def add(group_id, unit, place, half, fresh, piece, begin=False):
        if fresh:
            load(group_id, unit, place).wait()
        held = groups[group_id][0]
        count = held.shape[0] // 4
        part = jnp.dot(piece, held[place * count + unit], preferred_element_type=F32)
        part = part.reshape(half[1], own_rows, -1)
        if begin:
            part_of(accum, half)[...] = part
        else:
            part_of(accum, half)[...] += part

    def near_chunks(half, fresh):
        for group_id, (to_across, to_mate, forward, count) in enumerate(moves):
            source, got = sources[group_id][0], groups[group_id][2]
            if group_id == 0:
                add(0, 0, 0, half, fresh, read(source.at[0], half), True)
            else:
                each(count, lambda unit: add(group_id, unit, 0, half, fresh, read(source.at[unit], half)))

            def from_mate(unit):
                to_mate(unit, half).wait_recv()
                add(group_id, unit, 1, half, fresh, read(got.at[0, unit], half))

            each(count, from_mate)

    def far_chunks(half, fresh):
        for group_id, (to_across, to_mate, forward, count) in enumerate(moves):
            got = groups[group_id][2]

            def from_across(unit):
                to_across(unit, half).wait_recv()
                forward(unit, half).start()
                add(group_id, unit, 2, half, fresh, read(got.at[1, unit], half))
                forward(unit, half).wait_recv()
                add(group_id, unit, 3, half, fresh, read(got.at[2, unit], half))

            each(count, from_across)

    piece_wide = from_left.shape[-1]
    pieces = from_left.shape[1]

    def term(block, piece):
        return accum[block, :, piece * piece_wide : (piece + 1) * piece_wide]

    def to_right(block, piece):
        return remote(
            right_send.at[block, piece],
            from_left.at[block, piece],
            r_send.at[block, piece],
            r_recv.at[block, piece],
            {"rows": row + 1},
        )

    def to_left(block, piece):
        return remote(
            left_send.at[block, piece],
            from_right.at[block, piece],
            l_send.at[block, piece],
            l_recv.at[block, piece],
            {"rows": row - 1},
        )

    def run(move, send, arrived, block, edge):
        for piece in range(pieces):

            @pl.when(row == edge)
            def _():
                send[block, piece] = term(block, piece).astype(BF16)

            @pl.when(row != edge)
            def _():
                move(block, piece).wait_recv()
                send[block, piece] = (
                    term(block, piece) + arrived[block, piece].astype(F32)
                ).astype(BF16)

            move(block, piece).start()

    def run_right(block):
        run(to_right, right_send, from_left, block, 0)

    def run_left(block):
        run(to_left, left_send, from_right, block, row_count - 1)

    def send_far(from_end):
        at_end = (row == 0) | (row == row_count - 1)
        now = at_end if from_end else jnp.logical_not(at_end)

        @pl.when(now & (row < near))
        def _():
            each(near, lambda step: run_right(row_count - 1 - step))

        @pl.when(now & (row >= near))
        def _():
            each(near, run_left)

    near_chunks(stages[0], True)
    far_chunks(stages[0], True)
    send_far(True)
    if joint is not None:
        joint(home)
        share(stages[1])
        share(stages[2])
    near_chunks(stages[1], False)
    if has_up:
        far_chunks(stages[1], False)
        send_far(False)
        near_chunks(stages[2], False)
    else:
        far_chunks(stages[1], False)
        near_chunks(stages[2], False)
        send_far(False)

    @pl.when(row < pair)
    def _():
        run_right(pair)

    @pl.when(row > pair)
    def _():
        run_left(pair)

    far_chunks(stages[2], False)
    for piece in range(pieces):
        columns = slice(piece * piece_wide, (piece + 1) * piece_wide)
        total = term(row, piece) + base[:, columns].astype(F32)
        if has_up:
            total += bias[columns].reshape(1, -1)
        accum[row, :, columns] = total

        @pl.when(row > 0)
        def _():
            to_right(row, piece).wait_recv()
            accum[row, :, columns] += from_left[row, piece].astype(F32)

        @pl.when(row < row_count - 1)
        def _():
            to_left(row, piece).wait_recv()
            accum[row, :, columns] += from_right[row, piece].astype(F32)

        result[:, columns] = term(row, piece).astype(BF16)

    def sent(block):
        for piece in range(pieces):

            @pl.when(row < block)
            def _():
                to_right(block, piece).wait_send()

            @pl.when(row > block)
            def _():
                to_left(block, piece).wait_send()

    each(row_count, sent)

    for to_across, to_mate, forward, count in moves:

        def finish(unit):
            for half in stages:
                to_across(unit, half).wait_send()
                to_mate(unit, half).wait_send()
                forward(unit, half).wait_send()

        each(count, finish)


def out_scratch(groups, own_rows, width, row_count):
    dma = pltpu.SemaphoreType.DMA
    piece_wide = up_tile(width)
    pieces = width // piece_wide
    block = pltpu.VMEM((row_count, pieces, own_rows, piece_wide), BF16)
    scratch = [pltpu.VMEM((row_count, own_rows, width), F32)] + [block] * 4 + [dma((row_count, pieces))] * 4
    for count, piece in groups:
        scratch += [
            pltpu.VMEM((4 * count, piece, width), BF16),
            dma((4 * count,)),
            pltpu.VMEM((3, count, row_count, own_rows, piece), BF16),
            dma((count, 3)),
            dma((count, 3)),
            dma((count, 3)),
            dma((count, 3)),
            dma((2, count, 3)),
        ]
    return scratch


def out_call(name, number, base, heads, w_out, up=None):
    own_rows, width = base.shape
    _, half_rows, wide = heads.shape
    row_count = lax.axis_size("rows")
    any_spec, vmem_spec = pl.BlockSpec(memory_space=pl.ANY), pl.BlockSpec(memory_space=pltpu.VMEM)
    row_count = lax.axis_size("rows")
    operands = [base, heads.reshape(1, row_count, own_rows, wide), w_out]
    in_specs = [vmem_spec, vmem_spec, any_spec]
    groups = [(1, wide)]
    if up is not None:
        bias, hidden, w_down = up
        operands += [bias, hidden.reshape(hidden.shape[0], row_count, own_rows, -1), w_down]
        in_specs += [vmem_spec, vmem_spec, any_spec]
        groups.append((hidden.shape[0], hidden.shape[3]))
    scratch = out_scratch(groups, own_rows, width, row_count)
    return pl.pallas_call(
        functools.partial(out_kernel, up is not None),
        name=name,
        out_shape=jax.ShapeDtypeStruct((own_rows, width), BF16),
        in_specs=in_specs,
        out_specs=vmem_spec,
        scratch_shapes=scratch,
        compiler_params=pltpu.CompilerParams(
            collective_id=number, has_side_effects=True, vmem_limit_bytes=VMEM_LIMIT
        ),
    )(*operands)


def up_tile(columns):
    for tile in (4 * HEAD_DIM, 2 * HEAD_DIM, HEAD_DIM):
        if columns % tile == 0:
            return tile
    return columns


def kernel_body(
    camera_tokens,
    norm_gain,
    query_weight,
    key_weight,
    value_weight,
    query_gain,
    key_gain,
    out_weight,
    up_weight,
    up_bias,
    down_weight,
    down_bias,
    join_gain,
    join_query,
    join_key,
    join_value,
    join_query_gain,
    join_key_gain,
    join_out,
):
    all_rows = camera_tokens.shape[0] * lax.axis_size("rows")
    heads, hidden = in_call(
        "camera_in",
        0,
        TOK_CAM,
        camera_tokens,
        norm_gain,
        query_gain,
        key_gain,
        (query_weight, key_weight, value_weight),
        (up_bias, up_weight),
    )
    layer_own = out_call(
        "camera_out", 1, camera_tokens, heads, out_weight, (down_bias, hidden, down_weight)
    )
    return in_call(
        "join",
        2,
        all_rows,
        layer_own,
        join_gain,
        join_query_gain,
        join_key_gain,
        (join_query, join_key, join_value),
        join=join_out,
    )


def fits(mesh):
    cols, rows = mesh.shape["cols"], mesh.shape["rows"]
    return cols == 4 and rows == 4 and D % (rows * cols * HEAD_DIM) == 0


def solution(mesh):
    in_specs = (
        P(("groups", "rows"), "cols"),
        P("cols"),
        P("cols", "rows"),
        P("cols", "rows"),
        P("cols", "rows"),
        P("rows"),
        P("rows"),
        P("rows", "cols"),
        P("cols", "rows"),
        P("rows"),
        P("rows", "cols"),
        P("cols"),
        P("cols"),
        P("cols", "rows"),
        P("cols", "rows"),
        P("cols", "rows"),
        P("rows"),
        P("rows"),
        P("rows", "cols"),
    )
    out_specs = P(("groups", "rows"), "cols")
    body = kernel_body if fits(mesh) else plain_body
    return jax.shard_map(body, mesh=mesh, in_specs=in_specs, out_specs=out_specs, check_vma=False)
```
